32 devices in a mesh: dp: 8 (over y, x, core), mp: 4 (over z).
Axes of the slice: x: 2, y: 2, z: 4, core: 2. Of those that a mesh axis runs over, the one named last changes fastest.
Arguments:
- states: bfloat16 [512, 64, 256], P('dp', 'mp'), may hold values from -6 to 6
- key_embed: bfloat16 [512, 128], P('dp'), may hold values from -6 to 6
- partner: int32 [512], replicated, may hold values from 0 to 511, as said below
- mix_numer: int32 [512], P('dp'), may hold values from 1 to 15
- lengths: int32 [512], replicated, may hold values from 8 to 64
- w_qkv: bfloat16 [3, 256, 256], P(None, None, 'mp'), may hold values from -0.375 to 0.375
- w_out: bfloat16 [256, 256], P('mp'), may hold values from -0.375 to 0.375
- w_up: bfloat16 [256, 1024], P(None, 'mp'), may hold values from -0.375 to 0.375
- w_down: bfloat16 [1024, 256], P('mp'), may hold values from -0.1875 to 0.1875
- w_proj: bfloat16 [256, 128], replicated, may hold values from -0.375 to 0.375
Outputs:
- session_loss: float32 [512], P('dp')
- grad_states: float32 [512, 64, 256], P('dp', 'mp')
The draws below stay inside these ranges and needn't reach their ends.
Inputs may be any that keep to these rules, and one draw needn't show every extreme that they name: partner is a permutation of the 512 sessions; a session and its partner lie in different aligned blocks of 64 sessions, and at most 10 sessions of one block have their partners in one same other block.
All inputs are finite; a program needn't handle non-finite values.
Results may differ from the reference program's by a relative error of at most 0.0091.
Values may be sent and summed in bfloat16 or wider, within the bound.
A program may use at most 64 MiB of HBM per device.

```python
import jax
import jax.numpy as jnp
from jax import lax

D = 256
HEADS = 4
HD = 64
FF = 1024
E = 128
EV = 64
S_DEV = 64
INNER = 256
SESSIONS = 512
N_DP = 8


def draw_partner(key, part):
    base = jax.random.fold_in(key, 7)
    key_rank, key_slot, key_rows = jax.random.split(base, 3)
    ranks = jax.random.permutation(key_rank, S_DEV)
    shifts = 1 + ranks % (N_DP - 1)
    targets = jax.random.permutation(key_slot, S_DEV)
    row_keys = jax.random.split(key_rows, N_DP)
    orders = jax.vmap(lambda row_key: jax.random.permutation(row_key, S_DEV))(row_keys)
    devices = jnp.arange(N_DP, dtype=jnp.int32)[:, None]
    holder = (devices + shifts[orders]) % N_DP
    return (holder * S_DEV + targets[orders]).reshape(-1).astype(jnp.int32)


def touch_ends(entries, stream_key, smallest, largest):
    spot = [jax.random.randint(jax.random.fold_in(stream_key, axis), (), 0, length) for axis, length in enumerate(entries.shape)]
    widest = entries.shape.index(max(entries.shape))
    beside = spot[:widest] + [(spot[widest] + 1) % entries.shape[widest]] + spot[widest + 1:]
    return entries.at[tuple(spot)].set(smallest).at[tuple(beside)].set(largest)


def block_levels(rng, shape, cuts, least, largest):
    def one(dim, parts):
        steps = jax.random.uniform(jax.random.fold_in(jax.random.fold_in(rng, 6), dim), (parts,), jnp.float32, least / len(cuts), largest / len(cuts))
        return jnp.repeat(jnp.exp(steps), shape[dim] // parts).reshape((-1,) + (1,) * (len(shape) - dim - 1))

    gain = one(*cuts[0])
    for cut in cuts[1:]:
        gain = gain * one(*cut)
    return gain


def bell_draw(stream_key, extent, deviation, bound, cuts=(), kind=jnp.bfloat16):
    result = jax.random.normal(stream_key, extent, jnp.float32) * deviation
    if len(cuts) > 0:
        result = block_levels(stream_key, extent, cuts, -0.22, 0.18) * result
    return jnp.clip(result, min=-bound, max=bound).astype(kind)


def setup_inputs(seed: int = 0) -> dict:
    streams_of = jax.random.split(jax.random.key(seed), 11)
    states = bell_draw(streams_of[0], (SESSIONS, EV, D), 1.0, 6.0, ((0, 8), (1, 4)))
    key_embed = bell_draw(streams_of[1], (SESSIONS, E), 1.0, 6.0, ((0, 8),))
    partner = draw_partner(jax.random.fold_in(streams_of[10], 71), 0)
    mix_numer = touch_ends(jax.random.randint(streams_of[3], (SESSIONS,), 1, 16), jax.random.fold_in(streams_of[3], 1), 1, 15).astype(jnp.int32)
    lengths = touch_ends(jax.random.randint(streams_of[4], (SESSIONS,), EV // 8, EV + 1), jax.random.fold_in(streams_of[4], 1), EV // 8, EV).astype(jnp.int32)
    w_qkv = bell_draw(streams_of[5], (3, D, INNER), D ** -0.5, 0.375, ((2, 4),))
    w_out = bell_draw(streams_of[6], (INNER, D), INNER ** -0.5, 0.375, ((0, 4),))
    w_up = bell_draw(streams_of[7], (D, FF), D ** -0.5, 0.375, ((1, 4),))
    w_down = bell_draw(streams_of[8], (FF, D), FF ** -0.5, 0.1875, ((0, 4),))
    w_proj = bell_draw(streams_of[9], (D, E), D ** -0.5, 0.375)
    return dict(states=states, key_embed=key_embed, partner=partner, mix_numer=mix_numer, lengths=lengths, w_qkv=w_qkv, w_out=w_out, w_up=w_up, w_down=w_down, w_proj=w_proj)


SOFTMAX_TEMP = 0.1
LN_EPS = 1e-05
NORM_EPS = 1e-06
TOP_PRECISION = lax.Precision.HIGHEST

def rounded(values):
    return lax.optimization_barrier(values.astype(jnp.bfloat16)).astype(jnp.float32)

def layer_forward(mixed_blk, len_blk, w_qkv, w_out, w_up, w_down):
    block_size = mixed_blk.shape[0]
    row_mean = lax.optimization_barrier(jnp.mean(mixed_blk, axis=2, keepdims=True))
    centered = mixed_blk - row_mean
    inv_std = lax.rsqrt(lax.optimization_barrier(jnp.mean(centered * centered, axis=2, keepdims=True)) + LN_EPS)
    unit_rows = centered * inv_std
    normed = rounded(unit_rows)
    projected = rounded(jnp.einsum('btd,jdf->jbtf', normed, w_qkv.astype(jnp.float32)))
    projected = projected.reshape(3, block_size, EV, HEADS, HD)
    query_h = projected[0]
    key_h = projected[1]
    value_h = projected[2]
    score_scale = HD ** (-0.5)
    scores = jnp.einsum('bthc,brhc->bhtr', query_h, key_h) * score_scale
    positions = jnp.arange(EV, dtype=jnp.int32)
    token_mask = (positions[None, :] < len_blk[:, None]).astype(jnp.float32)
    exp_scores = jnp.exp(scores) * token_mask[:, None, None, :]
    probs = exp_scores / lax.optimization_barrier(jnp.sum(exp_scores, axis=3, keepdims=True))
    probs_b = rounded(probs)
    context = rounded(jnp.einsum('bhtr,brhc->bthc', probs_b, value_h)).reshape(block_size, EV, INNER)
    pre_act = jnp.einsum('btd,df->btf', normed, w_up.astype(jnp.float32))
    hidden = rounded(jax.nn.gelu(pre_act))
    branch = jnp.einsum('btf,fd->btd', context, w_out.astype(jnp.float32)) + jnp.einsum('btf,fd->btd', hidden, w_down.astype(jnp.float32))
    pool_weights = token_mask / len_blk[:, None].astype(jnp.float32)
    pooled = jnp.einsum('bt,btd->bd', pool_weights, mixed_blk + branch, precision=TOP_PRECISION)
    saved = (unit_rows, inv_std, query_h, key_h, value_h, probs, probs_b, pre_act, pool_weights)
    return (pooled, saved)

def layer_backward(mixed_blk, len_blk, grad_pooled, w_qkv, w_out, w_up, w_down):
    block_size = mixed_blk.shape[0]
    pooled, saved = layer_forward(mixed_blk, len_blk, w_qkv, w_out, w_up, w_down)
    unit_rows, inv_std, query_h, key_h, value_h, probs, probs_b, pre_act, pool_weights = saved
    grad_rows = grad_pooled[:, None, :] * pool_weights[:, :, None]
    grad_b = rounded(grad_rows)
    d_hidden = jnp.einsum('btd,fd->btf', grad_b, w_down.astype(jnp.float32))
    d_pre = rounded(jax.vjp(jax.nn.gelu, pre_act)[1](d_hidden)[0])
    d_context = rounded(jnp.einsum('btd,fd->btf', grad_b, w_out.astype(jnp.float32))).reshape(block_size, EV, HEADS, HD)
    d_value = rounded(jnp.einsum('bhtr,bthc->brhc', probs_b, d_context))
    d_prob = jnp.einsum('bthc,brhc->bhtr', d_context, value_h)
    d_score = rounded(probs * (d_prob - lax.optimization_barrier(jnp.sum(probs * d_prob, axis=3, keepdims=True))) * HD ** (-0.5))
    d_query = rounded(jnp.einsum('bhtr,brhc->bthc', d_score, key_h))
    d_key = rounded(jnp.einsum('bhtr,bthc->brhc', d_score, query_h))
    d_proj = jnp.stack([d_query, d_key, d_value]).reshape(3, block_size, EV, INNER)
    d_normed = jnp.einsum('jbtf,jdf->btd', d_proj, w_qkv.astype(jnp.float32)) + jnp.einsum('btf,df->btd', d_pre, w_up.astype(jnp.float32))
    center = lax.optimization_barrier(jnp.mean(d_normed, axis=2, keepdims=True))
    along = lax.optimization_barrier(jnp.mean(d_normed * unit_rows, axis=2, keepdims=True))
    return grad_rows + (d_normed - center - unit_rows * along) * inv_std

def reference(states, key_embed, partner, mix_numer, lengths, w_qkv, w_out, w_up, w_down, w_proj):
    mixup_weight = mix_numer.astype(jnp.float32) / 16.0
    mix_rows = mixup_weight[:, None, None]
    states_f = states.astype(jnp.float32)
    mixed = rounded(mix_rows * states_f + (1.0 - mix_rows) * states_f[partner])
    len_mix = jnp.maximum(lengths, lengths[partner])
    blocks_x = mixed.reshape(N_DP, S_DEV, EV, D)
    blocks_len = len_mix.reshape(N_DP, S_DEV)

    def forward_one(packed):
        return layer_forward(packed[0], packed[1], w_qkv, w_out, w_up, w_down)[0]
    pooled = lax.map(forward_one, (blocks_x, blocks_len)).reshape(SESSIONS, D)
    proj_f = w_proj.astype(jnp.float32)
    embed = jnp.dot(pooled, proj_f, precision=TOP_PRECISION)
    inv_norm = lax.rsqrt(lax.optimization_barrier(jnp.sum(embed * embed, axis=1, keepdims=True)) + NORM_EPS)
    unit_query_rows = embed * inv_norm
    keys_f = key_embed.astype(jnp.float32)
    unit_key_rows = keys_f * lax.rsqrt(lax.optimization_barrier(jnp.sum(keys_f * keys_f, axis=1, keepdims=True)) + NORM_EPS)
    pair_logits = jnp.dot(unit_query_rows, unit_key_rows.T, precision=TOP_PRECISION) / SOFTMAX_TEMP
    exp_logits = jnp.exp(pair_logits)
    sum_exp = lax.optimization_barrier(jnp.sum(exp_logits, axis=1))
    session_ids = jnp.arange(SESSIONS, dtype=jnp.int32)
    own_logit = jnp.take_along_axis(pair_logits, session_ids[:, None], axis=1)[:, 0]
    partner_logit = jnp.take_along_axis(pair_logits, partner[:, None], axis=1)[:, 0]
    session_loss = jnp.log(sum_exp) - mixup_weight * own_logit - (1.0 - mixup_weight) * partner_logit
    normalized_exponent = exp_logits / sum_exp[:, None]
    unit_gradient = (jnp.dot(normalized_exponent, unit_key_rows, precision=TOP_PRECISION) - mixup_weight[:, None] * unit_key_rows - (1.0 - mixup_weight)[:, None] * unit_key_rows[partner]) / SOFTMAX_TEMP
    grad_embed = (unit_gradient - unit_query_rows * lax.optimization_barrier(jnp.sum(unit_query_rows * unit_gradient, axis=1, keepdims=True))) * inv_norm
    grad_pooled = jnp.dot(grad_embed, proj_f.T, precision=TOP_PRECISION)

    def backward_one(packed):
        return layer_backward(packed[0], packed[1], packed[2], w_qkv, w_out, w_up, w_down)
    d_mixed = lax.map(backward_one, (blocks_x, blocks_len, grad_pooled.reshape(N_DP, S_DEV, D))).reshape(SESSIONS, EV, D)
    returned = rounded((1.0 - mix_rows) * d_mixed)
    inverse = jnp.argsort(partner).astype(jnp.int32)
    grad_states = mix_rows * d_mixed + returned[inverse]
    return (session_loss, grad_states)
```

```python
import functools

import jax
import jax.numpy as jnp
from jax import lax
from jax.experimental import pallas as pl
from jax.experimental.pallas import tpu as pltpu
from jax.sharding import PartitionSpec as P

HD = 64
SOFTMAX_TEMP = 0.1
LN_EPS = 1e-05
NORM_EPS = 1e-06
MESH = pl.DeviceIdType.MESH
F32 = jnp.float32
BF16 = jnp.bfloat16


def remote(src, dst, send_sem, recv_sem, device):
    return pltpu.make_async_remote_copy(
        src_ref=src,
        dst_ref=dst,
        send_sem=send_sem,
        recv_sem=recv_sem,
        device_id=device,
        device_id_type=MESH,
    )


def signal_all(n, mp):
    me, mz = lax.axis_index("dp"), lax.axis_index("mp")
    barrier = pltpu.get_barrier_semaphore()
    for o in range(1, n):
        pl.semaphore_signal(
            barrier, inc=1, device_id={"dp": lax.rem(me + o, n)}, device_id_type=MESH
        )
    for o in range(1, mp):
        pl.semaphore_signal(
            barrier, inc=1, device_id={"mp": lax.rem(mz + o, mp)}, device_id_type=MESH
        )


def wait_all(n, mp):
    pl.semaphore_wait(pltpu.get_barrier_semaphore(), n - 1 + mp - 1)


def dot(a, b, ca=1, cb=0):
    return lax.dot_general(
        a, b, (((ca,), (cb,)), ((), ())), preferred_element_type=F32
    )


def halves(a):
    hi = a.astype(BF16)
    return hi, (a - hi.astype(F32)).astype(BF16)


def dot_split(a, b, cb=0):
    hi, lo = halves(a)
    return dot(hi, b, 1, cb) + dot(lo, b, 1, cb)


def dot_both(a, b_hi, b_lo, cb=0):
    hi, lo = halves(a)
    return dot(hi, b_hi, 1, cb) + (dot(lo, b_hi, 1, cb) + dot(hi, b_lo, 1, cb))


def step_kernel(
    n, mp, group, cap, heads, nb,
    send_idx, recv_code, recv_idx, send_code, mix_num, lengths, partner,
    states, keys, w_qkv_in, w_out_in, w_up_in, w_down_in, w_proj,
    grad, loss_out,
    out_buf, in_lo, in_hi, mix_buf, mixed, all_keys, all_wts,
    dmix, dm_lo, dm_hi, ret_buf, arr_lo, arr_hi, loss, all_loss,
    wqkv, w_out, key_hi, key_lo, unit_s, inv_s, proj, probs, slope, hpool, xpool, ctx, seen_s,
    d_hid, d_ctx, g_row, aux, lens,
    dp_s, dp_r, key_s, key_r, mp_s, mp_r, wz_s, wz_r, wg_s, wg_r, wc_s, wc_r,
    zo_s, zo_r, ls_s, ls_r, do_s, do_r,
):
    me, mz = lax.axis_index("dp"), lax.axis_index("mp")
    in_buf = (in_lo, in_hi)
    dm_buf = (dm_lo, dm_hi)
    arr = (arr_lo, arr_hi)
    sessions, ev_part, width = states.shape
    half = width // 2
    chunk = sessions // mp
    pb = chunk // nb
    events = ev_part * mp
    part_w = w_out_in.shape[0]
    inner = part_w * mp
    ff_part = w_up_in.shape[1]
    ff = ff_part * mp
    lanes = heads * events
    rows_b = pb * events
    up0 = 4 * part_w
    down0 = up0 + width
    z_order = (2, 1, 3) if mp == 4 else tuple(range(1, mp))

    signal_all(n, mp)

    chips = group // 2
    piece = all_wts.shape[1] // group
    for j in range(3):
        all_wts[mz, j * part_w : (j + 1) * part_w, :] = w_qkv_in[j]
    all_wts[mz, 3 * part_w : 4 * part_w, :] = w_out_in[...]
    all_wts[mz, up0 : up0 + width, :] = w_up_in[...]
    all_wts[mz, down0:, :] = w_down_in[...]
    place = lax.rem(me, group)
    base = me - place
    core = lax.rem(place, 2)
    chip = place // 2
    core_rows = pl.ds(pl.multiple_of(core * (chips * piece), piece), chips * piece)
    rows = pl.ds(pl.multiple_of((core * chips + chip) * piece, piece), piece)

    @pl.loop(0, n * cap, unroll=8)
    def _(j):
        i = send_idx[j]
        for h in range(2):
            out_buf[h, j] = states[i, :, h * half : (h + 1) * half]

    wait_all(n, mp)

    pending = []
    dp = [[], []]
    for h in range(2):
        for o in range(1, n):
            peer = lax.rem(me + o, n)
            c = remote(
                out_buf.at[h, pl.ds(peer * cap, cap)], in_buf[h].at[pl.ds(me * cap, cap)],
                dp_s.at[h, o], dp_r.at[h, o], {"dp": peer},
            )
            c.start()
            dp[h].append(c)
    wz = []
    for o in range(1, mp):
        c = remote(
            all_wts.at[mz, rows], all_wts.at[mz, rows], wz_s.at[o], wz_r.at[o],
            {"mp": lax.rem(mz + o, mp)},
        )
        c.start()
        wz.append(c)
    key_rows = pl.ds(pl.multiple_of(me * sessions, sessions), sessions)
    key_copies = []
    for o in range(1, n):
        c = remote(
            keys, all_keys.at[key_rows], key_s.at[o], key_r.at[o], {"dp": lax.rem(me + o, n)}
        )
        c.start()
        key_copies.append(c)
    all_keys[key_rows, :] = keys[...]

    first = mz * chunk
    start = me * sessions + first
    for b in range(nb):
        for s in range(pb):
            i = b * pb + s
            other = partner[start + i]
            longest = jnp.maximum(lengths[start + i], lengths[other])
            lens[i] = longest
            row = slice(s, s + 1)
            shape = (1, aux.shape[3])
            aux[b, 0, row, :] = jnp.full(shape, mix_num[first + i].astype(F32) * 0.0625, F32)
            aux[b, 1, row, :] = jnp.full(shape, longest.astype(F32), F32)
            aux[b, 2, row, :] = jnp.full(shape, (start + i).astype(F32), F32)
            aux[b, 3, row, :] = jnp.full(shape, other.astype(F32), F32)

    def z_in(h, b, o):
        peer = lax.rem(mz + o, mp)
        return remote(
            mix_buf.at[h, pl.ds(peer * chunk + b * pb, pb)],
            mixed.at[pl.ds(b * pb, pb), mz, :, h * half : (h + 1) * half],
            mp_s.at[h, b, o], mp_r.at[h, b, o], {"mp": peer},
        )

    early = (nb + 1) // 2
    plane = []
    for h in range(2):
        cols = slice(h * half, (h + 1) * half)
        for c in dp[h]:
            c.wait()

        @pl.loop(0, sessions, unroll=8)
        def _(i):
            w = mix_num[i].astype(F32) * 0.0625
            mix_buf[h, i] = (
                w * states[i, :, cols].astype(F32)
                + (1.0 - w) * in_buf[h][recv_code[i]].astype(F32)
            ).astype(BF16)

        for b in range(early):
            for o in z_order:
                z_in(h, b, o).start()
        if h == 0:
            for o in range(1, mp):
                wz[o - 1].wait()
                held = lax.rem(mz + mp - o, mp)
                for g in range(1, chips):
                    peer = base + lax.rem(chip + g, chips) * 2 + core
                    c = remote(
                        all_wts.at[held, rows], all_wts.at[held, rows],
                        wg_s.at[o, g], wg_r.at[o, g], {"dp": peer},
                    )
                    c.start()
                    plane.append(c)
        else:
            for b in range(early, nb):
                for g in range(2):
                    for o in z_order:
                        z_in(g, b, o).start()

        @pl.loop(0, chunk, unroll=8)
        def _(i):
            mixed[i, mz, :, cols] = mix_buf[h, mz * chunk + i]

    for c in key_copies:
        c.wait()
    keys_f = all_keys[...].astype(F32)
    unit_k = keys_f * lax.rsqrt(jnp.sum(keys_f * keys_f, axis=1, keepdims=True) + NORM_EPS)
    k_hi, k_lo = halves(unit_k)
    key_hi[...] = k_hi
    key_lo[...] = k_lo

    for c in plane:
        c.wait()
    swap = []
    for o in range(1, mp):
        held = lax.rem(mz + mp - o, mp)
        c = remote(
            all_wts.at[held, core_rows], all_wts.at[held, core_rows],
            wc_s.at[o], wc_r.at[o], {"dp": me + 1 - 2 * core},
        )
        c.start()
        swap.append(c)
    for c in swap:
        c.wait()
    for m in range(mp):
        for j in range(3):
            wqkv[j * inner + m * part_w : j * inner + (m + 1) * part_w, :] = all_wts[
                m, j * part_w : (j + 1) * part_w, :
            ]
        w_out[m * part_w : (m + 1) * part_w, :] = all_wts[m, 3 * part_w : 4 * part_w, :]

    head_mask = (
        lax.broadcasted_iota(jnp.int32, (lanes, inner), 0) // events
        == lax.broadcasted_iota(jnp.int32, (lanes, inner), 1) // HD
    )
    ones_blk = head_mask.astype(F32).astype(BF16)
    row_t = lax.broadcasted_iota(jnp.int32, (events, lanes), 0)
    lane_t = lax.broadcasted_iota(jnp.int32, (events, lanes), 1) % events
    row_w = lax.broadcasted_iota(jnp.int32, (events, width), 0)
    col_head = lax.broadcasted_iota(jnp.int32, (events, inner), 1) // HD
    pool_row = lax.broadcasted_iota(jnp.int32, (pb, rows_b), 0)
    pool_lane = lax.broadcasted_iota(jnp.int32, (pb, rows_b), 1)
    zero_b = jnp.zeros((lanes, inner), BF16)
    scale = HD ** (-0.5)
    c0 = 0.7978845608028654
    c1 = c0 * 0.044715

    def spread(v):
        return jnp.where(head_mask, jnp.concatenate([v] * heads, axis=0), zero_b)

    def fold(full):
        total = full[0:events]
        for h in range(1, heads):
            total = jnp.where(col_head == h, full[h * events : (h + 1) * events], total)
        return total

    def forward(b):
        mixed_b = mixed[pl.ds(b * pb, pb)].reshape(rows_b, width)
        x = mixed_b.astype(F32)
        centered = x - jnp.mean(x, axis=1, keepdims=True)
        inv = lax.rsqrt(jnp.mean(centered * centered, axis=1, keepdims=True) + LN_EPS)
        unit = centered * inv
        unit_s[...] = unit
        inv_s[...] = jnp.broadcast_to(inv, inv_s.shape)
        normed = unit.astype(BF16)
        qkv = dot(normed, wqkv[...], 1, 1).astype(BF16)
        proj[...] = qkv
        len_col = aux[b, 1, :, 0:1]
        pool_mask = jnp.where(
            (pool_lane // events == pool_row)
            & ((pool_lane % events).astype(F32) < len_col),
            1.0,
            0.0,
        ).astype(BF16)
        xpool[...] = dot(pool_mask, mixed_b) / len_col
        for m in range(mp):
            pre = dot(normed, all_wts[m, up0 : up0 + width, :])
            sq = pre * pre
            side = 0.5 + 0.5 * jnp.tanh(pre * (c0 + c1 * sq))
            act = pre * side
            cols = slice(m * ff_part, (m + 1) * ff_part)
            slope[:, cols] = (
                side + act * (1.0 - side) * (2.0 * c0 + (6.0 * c1) * sq)
            ).astype(BF16)
            hpool[:, cols] = dot(pool_mask, act.astype(BF16)) / len_col
        used = []
        for s in range(pb):
            length = lens[b * pb + s]
            lo = s * events
            q = qkv[lo : lo + events, 0:inner]
            k = qkv[lo : lo + events, inner : 2 * inner]
            e = jnp.where(row_t < length, jnp.exp(dot(k, spread(q), 1, 1) * scale), 0.0)
            p = e * (1.0 / jnp.sum(e, axis=0, keepdims=True))
            probs[lo : lo + events, :] = p
            used.append(jnp.where(lane_t < length, p, 0.0).astype(BF16))
        seen = dot(jnp.concatenate(used, axis=0), ones_blk)
        seen_s[...] = seen
        for s in range(pb):
            lo = s * events
            v = qkv[lo : lo + events, 2 * inner : 3 * inner].astype(F32)
            ctx[s : s + 1, :] = jnp.sum(seen[lo : lo + events] * v, axis=0, keepdims=True) / lens[
                b * pb + s
            ].astype(F32)

    def contrast(b):
        weight, len_all = aux[b, 0, :, 0:1], aux[b, 1, :, 0:1]
        own_id, partner_id = aux[b, 2, :, 0:1], aux[b, 3, :, 0:1]
        pooled = xpool[...] + dot_split(ctx[...], w_out[...])
        for m in range(mp):
            cols = slice(m * ff_part, (m + 1) * ff_part)
            pooled = pooled + dot_split(hpool[:, cols], all_wts[m, down0 : down0 + ff_part, :])
        embed = dot_split(pooled, w_proj[...])
        inv_norm = lax.rsqrt(jnp.sum(embed * embed, axis=1, keepdims=True) + NORM_EPS)
        unit_q = embed * inv_norm
        logits = dot_both(unit_q, key_hi[...], key_lo[...], 1) / SOFTMAX_TEMP
        exp_l = jnp.exp(logits)
        sum_l = jnp.sum(exp_l, axis=1, keepdims=True)
        ids = lax.broadcasted_iota(jnp.int32, logits.shape, 1).astype(F32)
        wanted = jnp.where(ids == own_id, weight, 0.0) + jnp.where(
            ids == partner_id, 1.0 - weight, 0.0
        )
        loss[b] = jnp.broadcast_to(
            jnp.log(sum_l) - jnp.sum(wanted * logits, axis=1, keepdims=True), loss.shape[1:]
        )
        grad_u = dot_both(exp_l / sum_l - wanted, key_hi[...], key_lo[...]) / SOFTMAX_TEMP
        grad_e = (
            grad_u - unit_q * jnp.sum(unit_q * grad_u, axis=1, keepdims=True)
        ) * inv_norm
        g = dot_split(grad_e, w_proj[...], 1) * (1.0 / len_all)
        g_row[...] = g
        g_b = g.astype(BF16)
        for m in range(mp):
            d_hid[:, m * ff_part : (m + 1) * ff_part] = dot(
                g_b, all_wts[m, down0 : down0 + ff_part, :], 1, 1
            )
        d_ctx[...] = dot(g_b, w_out[...], 1, 1).astype(BF16).astype(F32)

    def backward(b):
        along_v = []
        for s in range(pb):
            lo = s * events
            v = proj[lo : lo + events, 2 * inner : 3 * inner].astype(F32)
            along_v.append((v * d_ctx[s : s + 1, :]).astype(BF16))
        u_all = dot(jnp.concatenate(along_v, axis=0), ones_blk, 1, 1)
        d_q, d_k, d_v = [], [], []
        for s in range(pb):
            length = lens[b * pb + s]
            lo = s * events
            q = proj[lo : lo + events, 0:inner]
            k = proj[lo : lo + events, inner : 2 * inner]
            p = probs[lo : lo + events, :]
            u = u_all[lo : lo + events]
            total = jnp.sum(p * u, axis=0, keepdims=True)
            d_score = jnp.where(lane_t < length, p * (u - total) * scale, 0.0).astype(BF16)
            d_k.append(dot(d_score, spread(q)).astype(BF16))
            d_q.append(fold(dot(d_score, k, 0, 0)).astype(BF16))
            d_v.append((seen_s[lo : lo + events, :] * d_ctx[s : s + 1, :]).astype(BF16))
        dn = dot(jnp.concatenate(d_q, axis=0), wqkv[0:inner, :])
        dn = dn + dot(jnp.concatenate(d_k, axis=0), wqkv[inner : 2 * inner, :])
        dn = dn + dot(jnp.concatenate(d_v, axis=0), wqkv[2 * inner : 3 * inner, :])
        for m in range(mp):
            cols = slice(m * ff_part, (m + 1) * ff_part)
            d_pre = jnp.concatenate(
                [
                    (
                        slope[s * events : (s + 1) * events, cols].astype(F32)
                        * d_hid[s : s + 1, cols]
                    ).astype(BF16)
                    for s in range(pb)
                ],
                axis=0,
            )
            dn = dn + dot(d_pre, all_wts[m, up0 : up0 + width, :], 1, 1)
        unit = unit_s[...]
        center = jnp.mean(dn, axis=1, keepdims=True)
        along = jnp.mean(dn * unit, axis=1, keepdims=True)
        body = (dn - center - unit * along) * inv_s[:, 0:1]
        for s in range(pb):
            d_mixed = jnp.where(
                row_w < lens[b * pb + s],
                g_row[s : s + 1, :] + body[s * events : (s + 1) * events],
                0.0,
            )
            dmix[b * pb + s] = d_mixed.astype(BF16).reshape(mp, ev_part, width)

    def z_out(h, b, o):
        peer = lax.rem(mz + o, mp)
        return remote(
            dmix.at[pl.ds(b * pb, pb), peer, :, h * half : (h + 1) * half],
            dm_buf[h].at[pl.ds(mz * chunk + b * pb, pb)],
            zo_s.at[h, b, o], zo_r.at[h, b, o], {"mp": peer},
        )

    @pl.loop(0, nb)
    def _(b):
        for h in range(2):
            for o in range(1, mp):
                z_in(h, b, o).wait()
        forward(b)
        contrast(b)
        backward(b)
        for h in range(2):
            for o in z_order:
                z_out(h, b, o).start()
        for s in range(pb):
            i = b * pb + s
            for h in range(2):
                dm_buf[h][mz * chunk + i] = dmix[i, mz, :, h * half : (h + 1) * half]

    for o in range(1, mp):
        c = remote(
            loss, all_loss.at[pl.ds(mz * nb, nb)],
            ls_s.at[o], ls_r.at[o], {"mp": lax.rem(mz + o, mp)},
        )
        c.start()
        pending.append(c)
    all_loss[pl.ds(mz * nb, nb)] = loss[...]

    back = [[], []]
    for h in range(2):
        for b in range(nb):
            for o in range(1, mp):
                z_out(h, b, o).wait()

        @pl.loop(0, n * cap, unroll=8)
        def _(j):
            i = recv_idx[j]
            ret_buf[h, j] = (
                (1.0 - mix_num[i].astype(F32) * 0.0625) * dm_buf[h][i].astype(F32)
            ).astype(BF16)

        for o in range(1, n):
            peer = lax.rem(me + o, n)
            c = remote(
                ret_buf.at[h, pl.ds(peer * cap, cap)], arr[h].at[pl.ds(me * cap, cap)],
                do_s.at[h, o], do_r.at[h, o], {"dp": peer},
            )
            c.start()
            back[h].append(c)
    for c in pending:
        c.wait()
    flat = all_loss[...].reshape(sessions, all_loss.shape[2])
    diagonal = lax.broadcasted_iota(
        jnp.int32, (sessions, sessions), 0
    ) == lax.broadcasted_iota(jnp.int32, (sessions, sessions), 1)
    loss_out[...] = jnp.sum(
        jnp.where(diagonal, flat[:, 0:sessions], 0.0), axis=0, keepdims=True
    )
    for h in range(2):
        for c in back[h]:
            c.wait()

        @pl.loop(0, sessions, unroll=8)
        def _(i):
            grad[i, :, h * half : (h + 1) * half] = (
                mix_num[i].astype(F32) * 0.0625 * dm_buf[h][i].astype(F32)
                + arr[h][send_code[i]].astype(F32)
            )


def local(states, key_embed, partner, mix_numer, lengths, w_qkv, w_out, w_up, w_down, w_proj):
    sessions, ev_part, width = states.shape
    n = lax.axis_size("dp")
    mp = lax.axis_size("mp")
    cap = (sessions + n - 2) // (n - 1)
    slots = n * cap
    me = lax.axis_index("dp")
    total = partner.shape[0]
    chunk = sessions // mp
    events = ev_part * mp
    inner_part = w_qkv.shape[2]
    inner = inner_part * mp
    heads = inner // HD
    ff_part = w_up.shape[1]
    group = 8 if n % 8 == 0 else 2
    half = width // 2

    source = partner.reshape(n, sessions) // sessions
    ids = jnp.arange(sessions, dtype=jnp.int32)
    slot = jnp.sum(
        (
            (source[:, :, None] == source[:, None, :]) & (ids[None, None, :] < ids[None, :, None])
        ).astype(jnp.int32),
        axis=2,
    )
    code = (jnp.arange(n, dtype=jnp.int32)[:, None] * cap + slot).reshape(-1)
    rel = partner - me * sessions
    slot_ids = jnp.arange(slots, dtype=jnp.int32)
    mine = (rel >= 0) & (rel < sessions)
    send_code = jnp.sum(jnp.where(rel[None, :] == ids[:, None], code[None, :], 0), axis=1)
    send_idx = jnp.sum(
        jnp.where((code[None, :] == slot_ids[:, None]) & mine[None, :], rel[None, :], 0), axis=1
    )
    own_source = lax.dynamic_slice_in_dim(source, me, 1, 0)[0]
    recv_code = own_source * cap + lax.dynamic_slice_in_dim(slot, me, 1, 0)[0]
    recv_idx = jnp.sum(
        jnp.where(recv_code[None, :] == slot_ids[:, None], ids[None, :], 0), axis=1
    )
    smem = pl.BlockSpec(memory_space=pltpu.SMEM)
    vmem = pl.BlockSpec(memory_space=pltpu.VMEM)
    dma = pltpu.SemaphoreType.DMA

    nb = 4 if chunk % 4 == 0 else 1
    pb = chunk // nb
    rows_b = pb * events
    lanes = heads * events
    ff = mp * ff_part
    embed = key_embed.shape[1]
    grad, loss_row = pl.pallas_call(
        functools.partial(step_kernel, n, mp, group, cap, heads, nb),
        out_shape=(
            jax.ShapeDtypeStruct((sessions, ev_part, width), F32),
            jax.ShapeDtypeStruct((1, sessions), F32),
        ),
        in_specs=[smem] * 7 + [vmem] * 7,
        out_specs=(vmem, vmem),
        scratch_shapes=[
            pltpu.VMEM((2, slots, ev_part, half), BF16),
            pltpu.VMEM((slots, ev_part, half), BF16),
            pltpu.VMEM((slots, ev_part, half), BF16),
            pltpu.VMEM((2, sessions, ev_part, half), BF16),
            pltpu.VMEM((chunk, mp, ev_part, width), BF16),
            pltpu.VMEM((total, embed), BF16),
            pltpu.VMEM((mp, 4 * inner_part + width + ff_part, width), BF16),
            pltpu.VMEM((chunk, mp, ev_part, width), BF16),
            pltpu.VMEM((sessions, ev_part, half), BF16),
            pltpu.VMEM((sessions, ev_part, half), BF16),
            pltpu.VMEM((2, slots, ev_part, half), BF16),
            pltpu.VMEM((slots, ev_part, half), BF16),
            pltpu.VMEM((slots, ev_part, half), BF16),
            pltpu.VMEM((nb, pb, 128), F32),
            pltpu.VMEM((mp * nb, pb, 128), F32),
            pltpu.VMEM((3 * inner, width), BF16),
            pltpu.VMEM((inner, width), BF16),
            pltpu.VMEM((total, embed), BF16),
            pltpu.VMEM((total, embed), BF16),
            pltpu.VMEM((rows_b, width), F32),
            pltpu.VMEM((rows_b, 128), F32),
            pltpu.VMEM((rows_b, 3 * inner), BF16),
            pltpu.VMEM((rows_b, lanes), F32),
            pltpu.VMEM((rows_b, ff), BF16),
            pltpu.VMEM((pb, ff), F32),
            pltpu.VMEM((pb, width), F32),
            pltpu.VMEM((pb, inner), F32),
            pltpu.VMEM((rows_b, inner), F32),
            pltpu.VMEM((pb, ff), F32),
            pltpu.VMEM((pb, inner), F32),
            pltpu.VMEM((pb, width), F32),
            pltpu.VMEM((nb, 4, pb, 128), F32),
            pltpu.SMEM((chunk,), jnp.int32),
            dma((2, n)), dma((2, n)), dma((n,)), dma((n,)),
            dma((2, nb, mp)), dma((2, nb, mp)), dma((mp,)), dma((mp,)),
            dma((mp, group)), dma((mp, group)), dma((mp,)), dma((mp,)),
            dma((2, nb, mp)), dma((2, nb, mp)), dma((mp,)), dma((mp,)),
            dma((2, n)), dma((2, n)),
        ],
        compiler_params=pltpu.CompilerParams(
            collective_id=0, has_side_effects=True, vmem_limit_bytes=56 * 1024 * 1024
        ),
    )(
        send_idx, recv_code, recv_idx, send_code, mix_numer, lengths, partner,
        states, key_embed, w_qkv.transpose(0, 2, 1), w_out, w_up, w_down, w_proj,
    )
    return (loss_row.reshape(sessions), grad)


def solution(mesh):
    placed = (
        P("dp", "mp", None),
        P("dp", None),
        P(),
        P("dp"),
        P(),
        P(None, None, "mp"),
        P("mp", None),
        P(None, "mp"),
        P("mp", None),
        P(),
    )
    return jax.shard_map(
        local, mesh=mesh, in_specs=placed, out_specs=(P("dp"), P("dp", "mp", None)), check_vma=False
    )
```

```python
import functools

import jax
import jax.numpy as jnp
from jax import lax
from jax.experimental import pallas as pl
from jax.experimental.pallas import tpu as pltpu
from jax.sharding import PartitionSpec as P

HD = 64
SOFTMAX_TEMP = 0.1
LN_EPS = 1e-05
NORM_EPS = 1e-06
MESH = pl.DeviceIdType.MESH
F32 = jnp.float32
BF16 = jnp.bfloat16


def remote(src, dst, send_sem, recv_sem, device):
    return pltpu.make_async_remote_copy(
        src_ref=src,
        dst_ref=dst,
        send_sem=send_sem,
        recv_sem=recv_sem,
        device_id=device,
        device_id_type=MESH,
    )


def signal_all(n, mp):
    me, mz = lax.axis_index("dp"), lax.axis_index("mp")
    barrier = pltpu.get_barrier_semaphore()
    for o in range(1, n):
        pl.semaphore_signal(
            barrier, inc=1, device_id={"dp": lax.rem(me + o, n)}, device_id_type=MESH
        )
    for o in range(1, mp):
        pl.semaphore_signal(
            barrier, inc=1, device_id={"mp": lax.rem(mz + o, mp)}, device_id_type=MESH
        )


def wait_all(n, mp):
    pl.semaphore_wait(pltpu.get_barrier_semaphore(), n - 1 + mp - 1)


def dot(a, b, ca=1, cb=0):
    return lax.dot_general(
        a, b, (((ca,), (cb,)), ((), ())), preferred_element_type=F32
    )


def halves(a):
    hi = a.astype(BF16)
    return hi, (a - hi.astype(F32)).astype(BF16)


def dot_split(a, b, cb=0):
    hi, lo = halves(a)
    return dot(hi, b, 1, cb) + dot(lo, b, 1, cb)


def dot_both(a, b_hi, b_lo, cb=0):
    hi, lo = halves(a)
    return dot(hi, b_hi, 1, cb) + (dot(lo, b_hi, 1, cb) + dot(hi, b_lo, 1, cb))


def step_kernel(
    n, mp, group, capb, heads, nb,
    send_idx, recv_code, recv_idx, send_code, order, home, mix_num, lengths, partner,
    states, keys, w_qkv_in, w_out_in, w_up_in, w_down_in, w_proj,
    grad, loss_out,
    out_buf, in_buf, in_now, mix_buf, mixed, all_keys, all_wts,
    dmix, dm_home, dm_now, ret_buf, arr, loss, all_loss,
    wqkv, w_out, key_hi, key_lo, unit_s, inv_s, proj, probs, slope, hpool, xpool, ctx, seen_s,
    d_hid, d_ctx, g_row, aux, lens,
    dp_s, dp_r, key_s, key_r, mp_s, mp_r, wz_s, wz_r, wg_s, wg_r, wc_s, wc_r,
    zo_s, zo_r, ls_s, ls_r, do_s, do_r,
):
    me, mz = lax.axis_index("dp"), lax.axis_index("mp")
    sessions, ev_part, width = states.shape
    chunk = sessions // mp
    pb = chunk // nb
    wave = mp * pb
    slots = n * capb
    events = ev_part * mp
    part_w = w_out_in.shape[0]
    inner = part_w * mp
    ff_part = w_up_in.shape[1]
    lanes = heads * events
    rows_b = pb * events
    up0 = 4 * part_w
    down0 = up0 + width
    z_order = (2, 1, 3) if mp == 4 else tuple(range(1, mp))

    signal_all(n, mp)

    chips = group // 2
    piece = all_wts.shape[1] // group
    for j in range(3):
        all_wts[mz, j * part_w : (j + 1) * part_w, :] = w_qkv_in[j]
    all_wts[mz, 3 * part_w : 4 * part_w, :] = w_out_in[...]
    all_wts[mz, up0 : up0 + width, :] = w_up_in[...]
    all_wts[mz, down0:, :] = w_down_in[...]
    place = lax.rem(me, group)
    base = me - place
    core = lax.rem(place, 2)
    chip = place // 2
    core_rows = pl.ds(pl.multiple_of(core * (chips * piece), piece), chips * piece)
    rows = pl.ds(pl.multiple_of((core * chips + chip) * piece, piece), piece)

    @pl.loop(0, nb * slots, unroll=8)
    def _(j):
        out_buf[j] = states[send_idx[j]]

    wait_all(n, mp)

    def dp_in(b, o):
        peer = lax.rem(me + o, n)
        return remote(
            out_buf.at[pl.ds(b * slots + peer * capb, capb)],
            in_buf.at[pl.ds(b * slots + me * capb, capb)],
            dp_s.at[b, o], dp_r.at[b, o], {"dp": peer},
        )

    def z_in(b, o):
        peer = lax.rem(mz + o, mp)
        return remote(
            mix_buf.at[pl.ds(b * wave + peer * pb, pb)],
            mixed.at[pl.ds(b * pb, pb), mz],
            mp_s.at[b, o], mp_r.at[b, o], {"mp": peer},
        )

    def z_out(b, o):
        peer = lax.rem(mz + o, mp)
        return remote(
            dmix.at[pl.ds(b * pb, pb), peer],
            dm_home.at[pl.ds(b * wave + mz * pb, pb)],
            zo_s.at[b, o], zo_r.at[b, o], {"mp": peer},
        )

    def dp_out(b, o):
        peer = lax.rem(me + o, n)
        return remote(
            ret_buf.at[pl.ds(b * slots + peer * capb, capb)],
            arr.at[pl.ds(b * slots + me * capb, capb)],
            do_s.at[b, o], do_r.at[b, o], {"dp": peer},
        )

    for b in range(nb):
        for o in range(1, n):
            dp_in(b, o).start()
    wz = []
    for o in range(1, mp):
        c = remote(
            all_wts.at[mz, rows], all_wts.at[mz, rows], wz_s.at[o], wz_r.at[o],
            {"mp": lax.rem(mz + o, mp)},
        )
        c.start()
        wz.append(c)
    key_rows = pl.ds(pl.multiple_of(me * sessions, sessions), sessions)
    key_copies = []
    for o in range(1, n):
        c = remote(
            keys, all_keys.at[key_rows], key_s.at[o], key_r.at[o], {"dp": lax.rem(me + o, n)}
        )
        c.start()
        key_copies.append(c)
    all_keys[key_rows, :] = keys[...]

    for b in range(nb):
        for s in range(pb):
            i = b * pb + s
            own = order[b * wave + mz * pb + s]
            other = partner[me * sessions + own]
            longest = jnp.maximum(lengths[me * sessions + own], lengths[other])
            lens[i] = longest
            row = slice(s, s + 1)
            shape = (1, aux.shape[3])
            aux[b, 0, row, :] = jnp.full(shape, mix_num[own].astype(F32) * 0.0625, F32)
            aux[b, 1, row, :] = jnp.full(shape, longest.astype(F32), F32)
            aux[b, 2, row, :] = jnp.full(shape, own.astype(F32), F32)
            aux[b, 3, row, :] = jnp.full(shape, other.astype(F32), F32)

    plane = []
    for b in range(nb):
        for o in range(1, n):
            dp_in(b, o).wait()
        in_now[...] = in_buf[pl.ds(b * slots, slots)]

        @pl.loop(0, wave, unroll=8)
        def _(t):
            i = order[b * wave + t]
            w = mix_num[i].astype(F32) * 0.0625
            mix_buf[b * wave + t] = (
                w * states[i].astype(F32)
                + (1.0 - w) * in_now[recv_code[b * wave + t]].astype(F32)
            ).astype(BF16)

        for o in z_order:
            z_in(b, o).start()
        mixed[b * pb : (b + 1) * pb, mz] = mix_buf[pl.ds(b * wave + mz * pb, pb)]
        if b == min(1, nb - 1):
            for o in range(1, mp):
                wz[o - 1].wait()
                held = lax.rem(mz + mp - o, mp)
                for g in range(1, chips):
                    peer = base + lax.rem(chip + g, chips) * 2 + core
                    c = remote(
                        all_wts.at[held, rows], all_wts.at[held, rows],
                        wg_s.at[o, g], wg_r.at[o, g], {"dp": peer},
                    )
                    c.start()
                    plane.append(c)

    for c in key_copies:
        c.wait()
    keys_f = all_keys[...].astype(F32)
    unit_k = keys_f * lax.rsqrt(jnp.sum(keys_f * keys_f, axis=1, keepdims=True) + NORM_EPS)
    k_hi, k_lo = halves(unit_k)
    key_hi[...] = k_hi
    key_lo[...] = k_lo

    for c in plane:
        c.wait()
    swap = []
    for o in range(1, mp):
        held = lax.rem(mz + mp - o, mp)
        c = remote(
            all_wts.at[held, core_rows], all_wts.at[held, core_rows],
            wc_s.at[o], wc_r.at[o], {"dp": me + 1 - 2 * core},
        )
        c.start()
        swap.append(c)
    for c in swap:
        c.wait()
    for m in range(mp):
        for j in range(3):
            wqkv[j * inner + m * part_w : j * inner + (m + 1) * part_w, :] = all_wts[
                m, j * part_w : (j + 1) * part_w, :
            ]
        w_out[m * part_w : (m + 1) * part_w, :] = all_wts[m, 3 * part_w : 4 * part_w, :]

    head_mask = (
        lax.broadcasted_iota(jnp.int32, (lanes, inner), 0) // events
        == lax.broadcasted_iota(jnp.int32, (lanes, inner), 1) // HD
    )
    ones_blk = head_mask.astype(F32).astype(BF16)
    row_t = lax.broadcasted_iota(jnp.int32, (events, lanes), 0)
    lane_t = lax.broadcasted_iota(jnp.int32, (events, lanes), 1) % events
    row_w = lax.broadcasted_iota(jnp.int32, (events, width), 0)
    col_head = lax.broadcasted_iota(jnp.int32, (events, inner), 1) // HD
    pool_row = lax.broadcasted_iota(jnp.int32, (pb, rows_b), 0)
    pool_lane = lax.broadcasted_iota(jnp.int32, (pb, rows_b), 1)
    zero_b = jnp.zeros((lanes, inner), BF16)
    scale = HD ** (-0.5)
    c0 = 0.7978845608028654
    c1 = c0 * 0.044715

    def spread(v):
        return jnp.where(head_mask, jnp.concatenate([v] * heads, axis=0), zero_b)

    def fold(full):
        total = full[0:events]
        for h in range(1, heads):
            total = jnp.where(col_head == h, full[h * events : (h + 1) * events], total)
        return total

    def forward(b):
        mixed_b = mixed[pl.ds(b * pb, pb)].reshape(rows_b, width)
        x = mixed_b.astype(F32)
        centered = x - jnp.mean(x, axis=1, keepdims=True)
        inv = lax.rsqrt(jnp.mean(centered * centered, axis=1, keepdims=True) + LN_EPS)
        unit = centered * inv
        unit_s[...] = unit
        inv_s[...] = jnp.broadcast_to(inv, inv_s.shape)
        normed = unit.astype(BF16)
        qkv = dot(normed, wqkv[...], 1, 1).astype(BF16)
        proj[...] = qkv
        len_col = aux[b, 1, :, 0:1]
        pool_mask = jnp.where(
            (pool_lane // events == pool_row)
            & ((pool_lane % events).astype(F32) < len_col),
            1.0,
            0.0,
        ).astype(BF16)
        xpool[...] = dot(pool_mask, mixed_b) / len_col
        for m in range(mp):
            pre = dot(normed, all_wts[m, up0 : up0 + width, :])
            sq = pre * pre
            side = 0.5 + 0.5 * jnp.tanh(pre * (c0 + c1 * sq))
            act = pre * side
            cols = slice(m * ff_part, (m + 1) * ff_part)
            slope[:, cols] = (
                side + act * (1.0 - side) * (2.0 * c0 + (6.0 * c1) * sq)
            ).astype(BF16)
            hpool[:, cols] = dot(pool_mask, act.astype(BF16)) / len_col
        used = []
        for s in range(pb):
            length = lens[b * pb + s]
            lo = s * events
            q = qkv[lo : lo + events, 0:inner]
            k = qkv[lo : lo + events, inner : 2 * inner]
            e = jnp.where(row_t < length, jnp.exp(dot(k, spread(q), 1, 1) * scale), 0.0)
            p = e * (1.0 / jnp.sum(e, axis=0, keepdims=True))
            probs[lo : lo + events, :] = p
            used.append(jnp.where(lane_t < length, p, 0.0).astype(BF16))
        seen = dot(jnp.concatenate(used, axis=0), ones_blk)
        seen_s[...] = seen
        for s in range(pb):
            lo = s * events
            v = qkv[lo : lo + events, 2 * inner : 3 * inner].astype(F32)
            ctx[s : s + 1, :] = jnp.sum(seen[lo : lo + events] * v, axis=0, keepdims=True) / lens[
                b * pb + s
            ].astype(F32)

    def contrast(b):
        weight, len_all = aux[b, 0, :, 0:1], aux[b, 1, :, 0:1]
        own, partner_id = aux[b, 2, :, 0:1], aux[b, 3, :, 0:1]
        own_id = own + (me * sessions).astype(F32)
        pooled = xpool[...] + dot_split(ctx[...], w_out[...])
        for m in range(mp):
            cols = slice(m * ff_part, (m + 1) * ff_part)
            pooled = pooled + dot_split(hpool[:, cols], all_wts[m, down0 : down0 + ff_part, :])
        embed = dot_split(pooled, w_proj[...])
        inv_norm = lax.rsqrt(jnp.sum(embed * embed, axis=1, keepdims=True) + NORM_EPS)
        unit_q = embed * inv_norm
        logits = dot_both(unit_q, key_hi[...], key_lo[...], 1) / SOFTMAX_TEMP
        exp_l = jnp.exp(logits)
        sum_l = jnp.sum(exp_l, axis=1, keepdims=True)
        ids = lax.broadcasted_iota(jnp.int32, logits.shape, 1).astype(F32)
        wanted = jnp.where(ids == own_id, weight, 0.0) + jnp.where(
            ids == partner_id, 1.0 - weight, 0.0
        )
        mine = lax.broadcasted_iota(jnp.int32, loss.shape[1:], 1).astype(F32) == own
        loss[b] = jnp.where(
            mine, jnp.log(sum_l) - jnp.sum(wanted * logits, axis=1, keepdims=True), 0.0
        )
        grad_u = dot_both(exp_l / sum_l - wanted, key_hi[...], key_lo[...]) / SOFTMAX_TEMP
        grad_e = (
            grad_u - unit_q * jnp.sum(unit_q * grad_u, axis=1, keepdims=True)
        ) * inv_norm
        g = dot_split(grad_e, w_proj[...], 1) * (1.0 / len_all)
        g_row[...] = g
        g_b = g.astype(BF16)
        for m in range(mp):
            d_hid[:, m * ff_part : (m + 1) * ff_part] = dot(
                g_b, all_wts[m, down0 : down0 + ff_part, :], 1, 1
            )
        d_ctx[...] = dot(g_b, w_out[...], 1, 1).astype(BF16).astype(F32)

    def backward(b):
        along_v = []
        for s in range(pb):
            lo = s * events
            v = proj[lo : lo + events, 2 * inner : 3 * inner].astype(F32)
            along_v.append((v * d_ctx[s : s + 1, :]).astype(BF16))
        u_all = dot(jnp.concatenate(along_v, axis=0), ones_blk, 1, 1)
        d_q, d_k, d_v = [], [], []
        for s in range(pb):
            length = lens[b * pb + s]
            lo = s * events
            q = proj[lo : lo + events, 0:inner]
            k = proj[lo : lo + events, inner : 2 * inner]
            p = probs[lo : lo + events, :]
            u = u_all[lo : lo + events]
            total = jnp.sum(p * u, axis=0, keepdims=True)
            d_score = jnp.where(lane_t < length, p * (u - total) * scale, 0.0).astype(BF16)
            d_k.append(dot(d_score, spread(q)).astype(BF16))
            d_q.append(fold(dot(d_score, k, 0, 0)).astype(BF16))
            d_v.append((seen_s[lo : lo + events, :] * d_ctx[s : s + 1, :]).astype(BF16))
        dn = dot(jnp.concatenate(d_q, axis=0), wqkv[0:inner, :])
        dn = dn + dot(jnp.concatenate(d_k, axis=0), wqkv[inner : 2 * inner, :])
        dn = dn + dot(jnp.concatenate(d_v, axis=0), wqkv[2 * inner : 3 * inner, :])
        for m in range(mp):
            cols = slice(m * ff_part, (m + 1) * ff_part)
            d_pre = jnp.concatenate(
                [
                    (
                        slope[s * events : (s + 1) * events, cols].astype(F32)
                        * d_hid[s : s + 1, cols]
                    ).astype(BF16)
                    for s in range(pb)
                ],
                axis=0,
            )
            dn = dn + dot(d_pre, all_wts[m, up0 : up0 + width, :], 1, 1)
        unit = unit_s[...]
        center = jnp.mean(dn, axis=1, keepdims=True)
        along = jnp.mean(dn * unit, axis=1, keepdims=True)
        body = (dn - center - unit * along) * inv_s[:, 0:1]
        for s in range(pb):
            d_mixed = jnp.where(
                row_w < lens[b * pb + s],
                g_row[s : s + 1, :] + body[s * events : (s + 1) * events],
                0.0,
            )
            dmix[b * pb + s] = d_mixed.astype(BF16).reshape(mp, ev_part, width)

    def give_back(b):
        for o in range(1, mp):
            z_out(b, o).wait()
        dm_now[...] = dm_home[pl.ds(b * wave, wave)]

        @pl.loop(0, slots, unroll=8)
        def _(j):
            t = recv_idx[b * slots + j]
            w = mix_num[order[b * wave + t]].astype(F32) * 0.0625
            ret_buf[b * slots + j] = ((1.0 - w) * dm_now[t].astype(F32)).astype(BF16)

        for o in range(1, n):
            dp_out(b, o).start()

    @pl.loop(0, nb)
    def _(b):
        for o in range(1, mp):
            z_in(b, o).wait()
        forward(b)
        contrast(b)
        backward(b)
        for o in z_order:
            z_out(b, o).start()
        dm_home[pl.ds(b * wave + mz * pb, pb)] = dmix[pl.ds(b * pb, pb), mz]

        @pl.when(b > 0)
        def _():
            give_back(b - 1)

    loss_copies = []
    for o in range(1, mp):
        c = remote(
            loss, all_loss.at[pl.ds(mz * nb, nb)],
            ls_s.at[o], ls_r.at[o], {"mp": lax.rem(mz + o, mp)},
        )
        c.start()
        loss_copies.append(c)
    all_loss[pl.ds(mz * nb, nb)] = loss[...]
    give_back(nb - 1)
    for c in loss_copies:
        c.wait()
    loss_out[...] = jnp.sum(jnp.sum(all_loss[...], axis=0), axis=0, keepdims=True)[:, 0:sessions]
    for b in range(nb):
        for o in range(1, n):
            dp_out(b, o).wait()

    @pl.loop(0, sessions, unroll=8)
    def _(i):
        grad[i] = (
            mix_num[i].astype(F32) * 0.0625 * dm_home[home[i]].astype(F32)
            + arr[send_code[i]].astype(F32)
        )


def local(states, key_embed, partner, mix_numer, lengths, w_qkv, w_out, w_up, w_down, w_proj):
    sessions, ev_part, width = states.shape
    n = lax.axis_size("dp")
    mp = lax.axis_size("mp")
    cap = (sessions + n - 2) // (n - 1)
    me = lax.axis_index("dp")
    total = partner.shape[0]
    chunk = sessions // mp
    nb = 4 if chunk % 4 == 0 else 1
    pb = chunk // nb
    wave = mp * pb
    capb = (cap + nb - 1) // nb
    slots = n * capb
    events = ev_part * mp
    inner_part = w_qkv.shape[2]
    inner = inner_part * mp
    heads = inner // HD
    ff_part = w_up.shape[1]
    group = 8 if n % 8 == 0 else 2

    source = partner.reshape(n, sessions) // sessions
    ids = jnp.arange(sessions, dtype=jnp.int32)
    same = (source[:, :, None] == source[:, None, :]) & (ids[None, None, :] < ids[None, :, None])
    slot = jnp.sum(same.astype(jnp.int32), axis=2)
    rank = slot + jnp.sum((source[:, None, :] < source[:, :, None]).astype(jnp.int32), axis=2)
    kind = (rank % nb) * slots + slot // nb
    place = (rank % nb) * wave + rank // nb
    code = (kind + jnp.arange(n, dtype=jnp.int32)[:, None] * capb).reshape(-1)
    rel = partner - me * sessions
    slot_ids = jnp.arange(nb * slots, dtype=jnp.int32)
    mine = (rel >= 0) & (rel < sessions)
    send_code = jnp.sum(jnp.where(rel[None, :] == ids[:, None], code[None, :], 0), axis=1)
    send_idx = jnp.sum(
        jnp.where((code[None, :] == slot_ids[:, None]) & mine[None, :], rel[None, :], 0), axis=1
    )
    home = lax.dynamic_slice_in_dim(place, me, 1, 0)[0]
    own_source = lax.dynamic_slice_in_dim(source, me, 1, 0)[0]
    own_kind = lax.dynamic_slice_in_dim(kind, me, 1, 0)[0]
    own_code = own_kind + own_source * capb
    at = home[None, :] == ids[:, None]
    order = jnp.sum(jnp.where(at, ids[None, :], 0), axis=1)
    recv_code = jnp.sum(jnp.where(at, own_code[None, :] % slots, 0), axis=1)
    recv_idx = jnp.sum(
        jnp.where(own_code[None, :] == slot_ids[:, None], home[None, :] % wave, 0), axis=1
    )
    smem = pl.BlockSpec(memory_space=pltpu.SMEM)
    vmem = pl.BlockSpec(memory_space=pltpu.VMEM)
    dma = pltpu.SemaphoreType.DMA

    rows_b = pb * events
    lanes = heads * events
    ff = mp * ff_part
    embed = key_embed.shape[1]
    grad, loss_row = pl.pallas_call(
        functools.partial(step_kernel, n, mp, group, capb, heads, nb),
        out_shape=(
            jax.ShapeDtypeStruct((sessions, ev_part, width), F32),
            jax.ShapeDtypeStruct((1, sessions), F32),
        ),
        in_specs=[smem] * 9 + [vmem] * 7,
        out_specs=(vmem, vmem),
        scratch_shapes=[
            pltpu.VMEM((nb * slots, ev_part, width), BF16),
            pltpu.VMEM((nb * slots, ev_part, width), BF16),
            pltpu.VMEM((slots, ev_part, width), BF16),
            pltpu.VMEM((sessions, ev_part, width), BF16),
            pltpu.VMEM((chunk, mp, ev_part, width), BF16),
            pltpu.VMEM((total, embed), BF16),
            pltpu.VMEM((mp, 4 * inner_part + width + ff_part, width), BF16),
            pltpu.VMEM((chunk, mp, ev_part, width), BF16),
            pltpu.VMEM((sessions, ev_part, width), BF16),
            pltpu.VMEM((wave, ev_part, width), BF16),
            pltpu.VMEM((nb * slots, ev_part, width), BF16),
            pltpu.VMEM((nb * slots, ev_part, width), BF16),
            pltpu.VMEM((nb, pb, 128), F32),
            pltpu.VMEM((mp * nb, pb, 128), F32),
            pltpu.VMEM((3 * inner, width), BF16),
            pltpu.VMEM((inner, width), BF16),
            pltpu.VMEM((total, embed), BF16),
            pltpu.VMEM((total, embed), BF16),
            pltpu.VMEM((rows_b, width), F32),
            pltpu.VMEM((rows_b, 128), F32),
            pltpu.VMEM((rows_b, 3 * inner), BF16),
            pltpu.VMEM((rows_b, lanes), F32),
            pltpu.VMEM((rows_b, ff), BF16),
            pltpu.VMEM((pb, ff), F32),
            pltpu.VMEM((pb, width), F32),
            pltpu.VMEM((pb, inner), F32),
            pltpu.VMEM((rows_b, inner), F32),
            pltpu.VMEM((pb, ff), F32),
            pltpu.VMEM((pb, inner), F32),
            pltpu.VMEM((pb, width), F32),
            pltpu.VMEM((nb, 4, pb, 128), F32),
            pltpu.SMEM((chunk,), jnp.int32),
            dma((nb, n)), dma((nb, n)), dma((n,)), dma((n,)),
            dma((nb, mp)), dma((nb, mp)), dma((mp,)), dma((mp,)),
            dma((mp, group)), dma((mp, group)), dma((mp,)), dma((mp,)),
            dma((nb, mp)), dma((nb, mp)), dma((mp,)), dma((mp,)),
            dma((nb, n)), dma((nb, n)),
        ],
        compiler_params=pltpu.CompilerParams(
            collective_id=0, has_side_effects=True, vmem_limit_bytes=56 * 1024 * 1024
        ),
    )(
        send_idx, recv_code, recv_idx, send_code, order, home, mix_numer, lengths, partner,
        states, key_embed, w_qkv.transpose(0, 2, 1), w_out, w_up, w_down, w_proj,
    )
    return (loss_row.reshape(sessions), grad)


def solution(mesh):
    placed = (
        P("dp", "mp", None),
        P("dp", None),
        P(),
        P("dp"),
        P(),
        P(None, None, "mp"),
        P("mp", None),
        P(None, "mp"),
        P("mp", None),
        P(),
    )
    return jax.shard_map(
        local, mesh=mesh, in_specs=placed, out_specs=(P("dp"), P("dp", "mp", None)), check_vma=False
    )
```

```python
import functools

import jax
import jax.numpy as jnp
from jax import lax
from jax.experimental import pallas as pl
from jax.experimental.pallas import tpu as pltpu
from jax.sharding import PartitionSpec as P

HD = 64
SOFTMAX_TEMP = 0.1
LN_EPS = 1e-05
NORM_EPS = 1e-06
MESH = pl.DeviceIdType.MESH
F32 = jnp.float32
BF16 = jnp.bfloat16


def remote(src, dst, send_sem, recv_sem, device):
    return pltpu.make_async_remote_copy(
        src_ref=src,
        dst_ref=dst,
        send_sem=send_sem,
        recv_sem=recv_sem,
        device_id=device,
        device_id_type=MESH,
    )


def signal_all(n, mp):
    me, mz = lax.axis_index("dp"), lax.axis_index("mp")
    barrier = pltpu.get_barrier_semaphore()
    for o in range(1, n):
        pl.semaphore_signal(
            barrier, inc=1, device_id={"dp": lax.rem(me + o, n)}, device_id_type=MESH
        )
    for o in range(1, mp):
        pl.semaphore_signal(
            barrier, inc=1, device_id={"mp": lax.rem(mz + o, mp)}, device_id_type=MESH
        )


def wait_all(n, mp):
    pl.semaphore_wait(pltpu.get_barrier_semaphore(), n - 1 + mp - 1)


def dot(a, b, ca=1, cb=0):
    return lax.dot_general(
        a, b, (((ca,), (cb,)), ((), ())), preferred_element_type=F32
    )


def halves(a):
    hi = a.astype(BF16)
    return hi, (a - hi.astype(F32)).astype(BF16)


def dot_split(a, b, cb=0):
    hi, lo = halves(a)
    return dot(hi, b, 1, cb) + dot(lo, b, 1, cb)


def dot_both(a, b_hi, b_lo, cb=0):
    hi, lo = halves(a)
    return dot(hi, b_hi, 1, cb) + (dot(lo, b_hi, 1, cb) + dot(hi, b_lo, 1, cb))


def over(x, k):
    return x >> (k.bit_length() - 1) if k & (k - 1) == 0 else x // k


def make_tables(n, mp, nb, capb, sessions, row_v, source_v, table_v):
    me = lax.axis_index("dp")
    slots = n * capb
    wave = sessions // nb
    lanes = table_v.shape[1]
    row = row_v[...]
    partner = jnp.concatenate(
        [row[:, d * sessions : (d + 1) * sessions] for d in range(n)], axis=0
    )
    source = over(partner, sessions)
    source_v[...] = source
    rel = partner - me * sessions
    mine = source == me
    i_sub = lax.broadcasted_iota(jnp.int32, (sessions, sessions), 0)
    i_lane = lax.broadcasted_iota(jnp.int32, (sessions, sessions), 1)
    here = jnp.where(mine, 1, 0)
    seen, step = here, 1
    while step < sessions:
        zeros = jnp.zeros((n, step), jnp.int32)
        seen = seen + jnp.concatenate([zeros, seen[:, : sessions - step]], axis=1)
        step *= 2
    slot = seen - here
    rank = slot + jnp.sum(jnp.where(source < me, 1, 0), axis=1, keepdims=True)
    wave_of = rank - over(rank, nb) * nb
    depth = over(slot, nb)
    cell = wave_of * capb + depth
    cell_lane = lax.broadcasted_iota(jnp.int32, (n, lanes), 1)
    send = jnp.zeros((n, lanes), jnp.int32)
    for c in range(nb * capb):
        value = jnp.sum(jnp.where(mine & (cell == c), rel, 0), axis=1, keepdims=True)
        send = jnp.where(cell_lane == c, value, send)
    table_v[8 : 8 + n, :] = jnp.clip(send, 0, sessions - 1)

    peer = lax.broadcasted_iota(jnp.int32, (n, sessions), 0)
    code = wave_of * slots + peer * capb + depth
    found = jnp.zeros((sessions, sessions), jnp.int32)
    for d in range(n):
        found = found + jnp.where(rel[d : d + 1] == i_sub, code[d : d + 1], 0)
    send_code = jnp.sum(found, axis=1, keepdims=True)

    own = source_v[pl.ds(me, 1), :]
    own_col = jnp.sum(jnp.where(i_sub == i_lane, own, 0), axis=1, keepdims=True)
    slot_col = jnp.sum(
        jnp.where((own_col == own) & (i_lane < i_sub), 1, 0), axis=1, keepdims=True
    )
    rank_col = slot_col + jnp.sum(jnp.where(own < own_col, 1, 0), axis=1, keepdims=True)
    t_col = over(rank_col, nb)
    b_col = rank_col - t_col * nb
    at_col = b_col * wave + t_col
    in_col = own_col * capb + over(slot_col, nb)
    code_col = b_col * slots + in_col
    wide_lane = lax.broadcasted_iota(jnp.int32, (sessions, lanes), 1)
    wide_sub = lax.broadcasted_iota(jnp.int32, (sessions, lanes), 0)

    def scatter(col, value, count):
        total = jnp.sum(jnp.where(col == wide_lane, value, 0), axis=0, keepdims=True)
        return jnp.clip(total, 0, count - 1)

    table_v[0:1, :] = scatter(at_col, wide_sub, sessions)
    table_v[1:2, :] = scatter(at_col, in_col, slots)
    table_v[2:3, :] = scatter(wide_sub, at_col, sessions)
    table_v[3:4, :] = scatter(wide_sub, send_code, nb * slots)
    table_v[4:5, :] = scatter(code_col, t_col, wave)
    table_v[5:8, :] = jnp.zeros((3, lanes), jnp.int32)


def step_kernel(
    n, mp, group, capb, heads, nb,
    partner_in, partner_row, lengths_in, mix_in,
    states_in, keys_in, w_qkv_in, w_out_in, w_up_in, w_down_in, w_proj_in,
    grad, loss_out,
    partner, lengths, mix_num, row_v, states, w_proj, source_v, table_v, table,
    out_buf, in_buf, in_now, mix_buf, mixed, all_keys, all_wts,
    dmix, dm_home, dm_now, ret_buf, arr, loss, all_loss,
    wqkv, w_out, key_hi, key_lo, unit_s, inv_s, proj, probs, slope, hpool, xpool, ctx, seen_s,
    d_hid, d_ctx, g_row, aux, lens,
    dp_s, dp_r, key_s, key_r, mp_s, mp_r, wz_s, wz_r, wg_s, wg_r, wc_s, wc_r,
    zo_s, zo_r, ls_s, ls_r, do_s, do_r, in_sem, w_sem, table_sem,
):
    me, mz = lax.axis_index("dp"), lax.axis_index("mp")
    sessions, ev_part, width = states.shape
    chunk = sessions // mp
    pb = chunk // nb
    wave = mp * pb
    slots = n * capb
    events = ev_part * mp
    part_w = w_out_in.shape[0]
    inner = part_w * mp
    ff_part = w_up_in.shape[1]
    lanes = heads * events
    rows_b = pb * events
    up0 = 4 * part_w
    down0 = up0 + width
    z_order = (2, 1, 3) if mp == 4 else tuple(range(1, mp))

    signal_all(n, mp)

    chips = group // 2
    place = lax.rem(me, group)
    base = me - place
    core = lax.rem(place, 2)
    chip = place // 2
    key_rows = pl.ds(pl.multiple_of(me * sessions, sessions), sessions)
    loads = [
        pltpu.make_async_copy(src, dst, in_sem.at[i])
        for i, (src, dst) in enumerate(
            [
                (partner_row, row_v),
                (partner_in, partner),
                (lengths_in, lengths),
                (mix_in, mix_num),
                (states_in, states),
                (keys_in, all_keys.at[key_rows]),
                (w_proj_in, w_proj),
            ]
        )
    ]
    w_loads = [
        pltpu.make_async_copy(src, all_wts.at[mz, pl.ds(at, src.shape[0])], w_sem.at[i])
        for i, (src, at) in enumerate(
            [(w_qkv_in.at[j], j * part_w) for j in range(3)]
            + [(w_out_in, 3 * part_w), (w_up_in, up0), (w_down_in, down0)]
        )
    ]
    loads[0].start()
    for c in w_loads:
        c.start()
    for c in loads[1:]:
        c.start()
    loads[0].wait()
    make_tables(n, mp, nb, capb, sessions, row_v, source_v, table_v)
    table_copy = pltpu.make_async_copy(table_v, table, table_sem)
    table_copy.start()

    def order(p):
        return table[0, p]

    for c in w_loads:
        c.wait()
    loads[5].wait()
    wait_all(n, mp)

    def dp_in(b, o):
        peer = lax.rem(me + o, n)
        return remote(
            out_buf.at[pl.ds(b * slots + peer * capb, capb)],
            in_buf.at[pl.ds(b * slots + me * capb, capb)],
            dp_s.at[b, o], dp_r.at[b, o], {"dp": peer},
        )

    def z_in(b, o):
        peer = lax.rem(mz + o, mp)
        return remote(
            mix_buf.at[pl.ds(b * wave + peer * pb, pb)],
            mixed.at[pl.ds(b * pb, pb), mz],
            mp_s.at[b, o], mp_r.at[b, o], {"mp": peer},
        )

    def z_out(b, o):
        peer = lax.rem(mz + o, mp)
        return remote(
            dmix.at[pl.ds(b * pb, pb), peer],
            dm_home.at[pl.ds(b * wave + mz * pb, pb)],
            zo_s.at[b, o], zo_r.at[b, o], {"mp": peer},
        )

    def dp_out(b, o):
        peer = lax.rem(me + o, n)
        return remote(
            ret_buf.at[pl.ds(b * slots + peer * capb, capb)],
            arr.at[pl.ds(b * slots + me * capb, capb)],
            do_s.at[b, o], do_r.at[b, o], {"dp": peer},
        )

    sizes = (4 * part_w, width, ff_part)
    offsets = (0, up0, down0)

    def w_rows(g, first, count):
        piece = sizes[g] // group
        return pl.ds(pl.multiple_of(offsets[g] + first * piece, piece), count * piece)

    def w_z(g, o):
        part = all_wts.at[mz, w_rows(g, core * chips + chip, 1)]
        return remote(part, part, wz_s.at[g, o], wz_r.at[g, o], {"mp": lax.rem(mz + o, mp)})

    def w_plane(g, o, h):
        part = all_wts.at[lax.rem(mz + mp - o, mp), w_rows(g, core * chips + chip, 1)]
        peer = base + lax.rem(chip + h, chips) * 2 + core
        return remote(part, part, wg_s.at[g, o, h], wg_r.at[g, o, h], {"dp": peer})

    def w_core(g, o):
        part = all_wts.at[lax.rem(mz + mp - o, mp), w_rows(g, core * chips, chips)]
        return remote(part, part, wc_s.at[g, o], wc_r.at[g, o], {"dp": me + 1 - 2 * core})

    def spread_weights(g):
        for o in range(1, mp):
            w_z(g, o).wait()
            for h in range(1, chips):
                w_plane(g, o, h).start()

    def swap_weights(g):
        for o in range(1, mp):
            for h in range(1, chips):
                w_plane(g, o, h).wait()
            w_core(g, o).start()

    def have_weights(g):
        for o in range(1, mp):
            w_core(g, o).wait()

    def send_out(b):
        @pl.loop(0, n, unroll=2)
        def _(d):
            for k in range(capb):
                out_buf[b * slots + d * capb + k] = states[table[8 + d, b * capb + k]]

        for o in range(1, n):
            dp_in(b, o).start()

    def mix(b):
        for o in range(1, n):
            dp_in(b, o).wait()
        in_now[...] = in_buf[pl.ds(b * slots, slots)]

        @pl.loop(0, wave, unroll=8)
        def _(t):
            i = order(b * wave + t)
            w = mix_num[i].astype(F32) * 0.0625
            mix_buf[b * wave + t] = (
                w * states[i].astype(F32)
                + (1.0 - w) * in_now[table[1, b * wave + t]].astype(F32)
            ).astype(BF16)

        for o in z_order:
            z_in(b, o).start()
        mixed[b * pb : (b + 1) * pb, mz] = mix_buf[pl.ds(b * wave + mz * pb, pb)]

    key_copies = [
        remote(
            all_keys.at[key_rows], all_keys.at[key_rows], key_s.at[o], key_r.at[o],
            {"dp": lax.rem(me + o, n)},
        )
        for o in range(1, n)
    ]
    for g in range(3):
        for o in range(1, mp):
            w_z(g, o).start()
    for c in loads[1:5] + loads[6:]:
        c.wait()
    table_copy.wait()
    ahead = min(2, nb)
    for b in range(ahead):
        send_out(b)
    for b in range(nb):
        for s in range(pb):
            i = b * pb + s
            own = order(b * wave + mz * pb + s)
            other = partner[me * sessions + own]
            longest = jnp.maximum(lengths[me * sessions + own], lengths[other])
            lens[i] = longest
            row = slice(s, s + 1)
            shape = (1, aux.shape[3])
            aux[b, 0, row, :] = jnp.full(shape, mix_num[own].astype(F32) * 0.0625, F32)
            aux[b, 1, row, :] = jnp.full(shape, longest.astype(F32), F32)
            aux[b, 2, row, :] = jnp.full(shape, own.astype(F32), F32)
            aux[b, 3, row, :] = jnp.full(shape, other.astype(F32), F32)
    spread_weights(0)
    mix(0)
    spread_weights(1)
    mix(1)
    spread_weights(2)
    for c in key_copies:
            c.start()
    for b in range(ahead, nb):
            send_out(b)
    swap_weights(0)

    head_mask = (
        lax.broadcasted_iota(jnp.int32, (lanes, inner), 0) // events
        == lax.broadcasted_iota(jnp.int32, (lanes, inner), 1) // HD
    )
    ones_blk = head_mask.astype(F32).astype(BF16)
    row_t = lax.broadcasted_iota(jnp.int32, (events, lanes), 0)
    lane_t = lax.broadcasted_iota(jnp.int32, (events, lanes), 1) % events
    row_w = lax.broadcasted_iota(jnp.int32, (events, width), 0)
    col_head = lax.broadcasted_iota(jnp.int32, (events, inner), 1) // HD
    pool_row = lax.broadcasted_iota(jnp.int32, (pb, rows_b), 0)
    pool_lane = lax.broadcasted_iota(jnp.int32, (pb, rows_b), 1)
    zero_b = jnp.zeros((lanes, inner), BF16)
    scale = HD ** (-0.5)
    c0 = 0.7978845608028654
    c1 = c0 * 0.044715

    def spread(v):
        return jnp.where(head_mask, jnp.concatenate([v] * heads, axis=0), zero_b)

    def fold(full):
        total = full[0:events]
        for h in range(1, heads):
            total = jnp.where(col_head == h, full[h * events : (h + 1) * events], total)
        return total

    def attend(b):
        mixed_b = mixed[pl.ds(b * pb, pb)].reshape(rows_b, width)
        x = mixed_b.astype(F32)
        centered = x - jnp.mean(x, axis=1, keepdims=True)
        inv = lax.rsqrt(jnp.mean(centered * centered, axis=1, keepdims=True) + LN_EPS)
        unit = centered * inv
        unit_s[b] = unit
        inv_s[b] = jnp.broadcast_to(inv, inv_s.shape[1:])
        qkv = dot(unit.astype(BF16), wqkv[...], 1, 1).astype(BF16)
        proj[b] = qkv
        used = []
        for s in range(pb):
            length = lens[b * pb + s]
            lo = s * events
            q = qkv[lo : lo + events, 0:inner]
            k = qkv[lo : lo + events, inner : 2 * inner]
            e = jnp.where(row_t < length, jnp.exp(dot(k, spread(q), 1, 1) * scale), 0.0)
            p = e * (1.0 / jnp.sum(e, axis=0, keepdims=True))
            probs[b, lo : lo + events, :] = p
            used.append(jnp.where(lane_t < length, p, 0.0).astype(BF16))
        seen = dot(jnp.concatenate(used, axis=0), ones_blk)
        seen_s[b] = seen
        for s in range(pb):
            lo = s * events
            v = qkv[lo : lo + events, 2 * inner : 3 * inner].astype(F32)
            ctx[b, s : s + 1, :] = jnp.sum(
                seen[lo : lo + events] * v, axis=0, keepdims=True
            ) / lens[b * pb + s].astype(F32)

    def feed(b):
        len_col = aux[b, 1, :, 0:1]
        pool_mask = jnp.where(
            (pool_lane // events == pool_row)
            & ((pool_lane % events).astype(F32) < len_col),
            1.0,
            0.0,
        ).astype(BF16)
        xpool[...] = dot(pool_mask, mixed[pl.ds(b * pb, pb)].reshape(rows_b, width)) / len_col
        normed = unit_s[b].astype(BF16)
        for m in range(mp):
            pre = dot(normed, all_wts[m, up0 : up0 + width, :])
            sq = pre * pre
            side = 0.5 + 0.5 * jnp.tanh(pre * (c0 + c1 * sq))
            act = pre * side
            cols = slice(m * ff_part, (m + 1) * ff_part)
            slope[:, cols] = (
                side + act * (1.0 - side) * (2.0 * c0 + (6.0 * c1) * sq)
            ).astype(BF16)
            hpool[:, cols] = dot(pool_mask, act.astype(BF16)) / len_col

    def contrast(b):
        weight, len_all = aux[b, 0, :, 0:1], aux[b, 1, :, 0:1]
        own, partner_id = aux[b, 2, :, 0:1], aux[b, 3, :, 0:1]
        own_id = own + (me * sessions).astype(F32)
        pooled = xpool[...] + dot_split(ctx[b], w_out[...])
        for m in range(mp):
            cols = slice(m * ff_part, (m + 1) * ff_part)
            pooled = pooled + dot_split(hpool[:, cols], all_wts[m, down0 : down0 + ff_part, :])
        embed = dot_split(pooled, w_proj[...])
        inv_norm = lax.rsqrt(jnp.sum(embed * embed, axis=1, keepdims=True) + NORM_EPS)
        unit_q = embed * inv_norm
        logits = dot_both(unit_q, key_hi[...], key_lo[...], 1) / SOFTMAX_TEMP
        exp_l = jnp.exp(logits)
        sum_l = jnp.sum(exp_l, axis=1, keepdims=True)
        ids = lax.broadcasted_iota(jnp.int32, logits.shape, 1).astype(F32)
        wanted = jnp.where(ids == own_id, weight, 0.0) + jnp.where(
            ids == partner_id, 1.0 - weight, 0.0
        )
        mine = lax.broadcasted_iota(jnp.int32, loss.shape[1:], 1).astype(F32) == own
        loss[b] = jnp.where(
            mine, jnp.log(sum_l) - jnp.sum(wanted * logits, axis=1, keepdims=True), 0.0
        )
        grad_u = dot_both(exp_l / sum_l - wanted, key_hi[...], key_lo[...]) / SOFTMAX_TEMP
        grad_e = (
            grad_u - unit_q * jnp.sum(unit_q * grad_u, axis=1, keepdims=True)
        ) * inv_norm
        g = dot_split(grad_e, w_proj[...], 1) * (1.0 / len_all)
        g_row[...] = g
        g_b = g.astype(BF16)
        for m in range(mp):
            d_hid[:, m * ff_part : (m + 1) * ff_part] = dot(
                g_b, all_wts[m, down0 : down0 + ff_part, :], 1, 1
            )
        d_ctx[...] = dot(g_b, w_out[...], 1, 1).astype(BF16).astype(F32)

    def backward(b):
        along_v = []
        for s in range(pb):
            lo = s * events
            v = proj[b, lo : lo + events, 2 * inner : 3 * inner].astype(F32)
            along_v.append((v * d_ctx[s : s + 1, :]).astype(BF16))
        u_all = dot(jnp.concatenate(along_v, axis=0), ones_blk, 1, 1)
        d_q, d_k, d_v = [], [], []
        for s in range(pb):
            length = lens[b * pb + s]
            lo = s * events
            q = proj[b, lo : lo + events, 0:inner]
            k = proj[b, lo : lo + events, inner : 2 * inner]
            p = probs[b, lo : lo + events, :]
            u = u_all[lo : lo + events]
            total = jnp.sum(p * u, axis=0, keepdims=True)
            d_score = jnp.where(lane_t < length, p * (u - total) * scale, 0.0).astype(BF16)
            d_k.append(dot(d_score, spread(q)).astype(BF16))
            d_q.append(fold(dot(d_score, k, 0, 0)).astype(BF16))
            d_v.append((seen_s[b, lo : lo + events, :] * d_ctx[s : s + 1, :]).astype(BF16))
        dn = dot(jnp.concatenate(d_q, axis=0), wqkv[0:inner, :])
        dn = dn + dot(jnp.concatenate(d_k, axis=0), wqkv[inner : 2 * inner, :])
        dn = dn + dot(jnp.concatenate(d_v, axis=0), wqkv[2 * inner : 3 * inner, :])
        for m in range(mp):
            cols = slice(m * ff_part, (m + 1) * ff_part)
            d_pre = jnp.concatenate(
                [
                    (
                        slope[s * events : (s + 1) * events, cols].astype(F32)
                        * d_hid[s : s + 1, cols]
                    ).astype(BF16)
                    for s in range(pb)
                ],
                axis=0,
            )
            dn = dn + dot(d_pre, all_wts[m, up0 : up0 + width, :], 1, 1)
        unit = unit_s[b]
        center = jnp.mean(dn, axis=1, keepdims=True)
        along = jnp.mean(dn * unit, axis=1, keepdims=True)
        body = (dn - center - unit * along) * inv_s[b, :, 0:1]
        for s in range(pb):
            d_mixed = jnp.where(
                row_w < lens[b * pb + s],
                g_row[s : s + 1, :] + body[s * events : (s + 1) * events],
                0.0,
            )
            dmix[b * pb + s] = d_mixed.astype(BF16).reshape(mp, ev_part, width)

    def give_back(b):
        for o in range(1, mp):
            z_out(b, o).wait()
        dm_now[...] = dm_home[pl.ds(b * wave, wave)]

        @pl.loop(0, slots, unroll=8)
        def _(j):
            t = table[4, b * slots + j]
            w = mix_num[order(b * wave + t)].astype(F32) * 0.0625
            ret_buf[b * slots + j] = ((1.0 - w) * dm_now[t].astype(F32)).astype(BF16)

        for o in range(1, n):
            dp_out(b, o).start()

    def arrived(b):
        for o in range(1, mp):
            z_in(b, o).wait()

    have_weights(0)
    for m in range(mp):
        for j in range(3):
            wqkv[j * inner + m * part_w : j * inner + (m + 1) * part_w, :] = all_wts[
                m, j * part_w : (j + 1) * part_w, :
            ]
        w_out[m * part_w : (m + 1) * part_w, :] = all_wts[m, 3 * part_w : 4 * part_w, :]
    arrived(0)
    attend(0)
    swap_weights(1)
    for b in range(ahead, min(3, nb)):
        mix(b)
    if nb > 1:
        arrived(1)
        attend(1)
    swap_weights(2)
    for b in range(3, nb):
        mix(b)
    for c in key_copies:
        c.wait()
    keys_f = all_keys[...].astype(F32)
    unit_k = keys_f * lax.rsqrt(jnp.sum(keys_f * keys_f, axis=1, keepdims=True) + NORM_EPS)
    k_hi, k_lo = halves(unit_k)
    key_hi[...] = k_hi
    key_lo[...] = k_lo
    have_weights(1)
    have_weights(2)

    for b in range(nb):
        feed(b)
        contrast(b)
        backward(b)
        for o in z_order:
            z_out(b, o).start()
        dm_home[pl.ds(b * wave + mz * pb, pb)] = dmix[pl.ds(b * pb, pb), mz]
        if b + ahead < nb:
            arrived(b + ahead)
            attend(b + ahead)
        if b > 0:
            give_back(b - 1)

    loss_copies = []
    for o in range(1, mp):
        c = remote(
            loss, all_loss.at[pl.ds(mz * nb, nb)],
            ls_s.at[o], ls_r.at[o], {"mp": lax.rem(mz + o, mp)},
        )
        c.start()
        loss_copies.append(c)
    all_loss[pl.ds(mz * nb, nb)] = loss[...]
    give_back(nb - 1)
    for c in loss_copies:
        c.wait()
    loss_out[...] = jnp.sum(jnp.sum(all_loss[...], axis=0), axis=0, keepdims=True)
    for b in range(nb):
        for o in range(1, n):
            dp_out(b, o).wait()

    @pl.loop(0, sessions, unroll=8)
    def _(i):
        grad[i] = (
            mix_num[i].astype(F32) * 0.0625 * dm_home[table[2, i]].astype(F32)
            + arr[table[3, i]].astype(F32)
        )


def hand_over(parts, grad_in, loss_in, grad, loss, held, in_sem, out_sem):
    block = grad.shape[0] // parts
    ins, outs = [], []
    for i in range(parts):
        rows = pl.ds(i * block, block)
        ins.append(pltpu.make_async_copy(grad_in.at[rows], held.at[rows], in_sem.at[i]))
        outs.append(pltpu.make_async_copy(held.at[rows], grad.at[rows], out_sem.at[i]))
        ins[i].start()
    loss[...] = loss_in[:, 0 : loss.shape[1]]
    for i in range(parts):
        ins[i].wait()
        outs[i].start()
    for i in range(parts):
        outs[i].wait()


def local(states, key_embed, partner, mix_numer, lengths, w_qkv, w_out, w_up, w_down, w_proj):
    sessions, ev_part, width = states.shape
    n = lax.axis_size("dp")
    mp = lax.axis_size("mp")
    cap = (sessions + n - 2) // (n - 1)
    me = lax.axis_index("dp")
    total = partner.shape[0]
    chunk = sessions // mp
    nb = 4 if chunk % 4 == 0 else 1
    pb = chunk // nb
    wave = mp * pb
    capb = (cap + nb - 1) // nb
    slots = n * capb
    events = ev_part * mp
    inner_part = w_qkv.shape[2]
    inner = inner_part * mp
    heads = inner // HD
    ff_part = w_up.shape[1]
    group = 8 if n % 8 == 0 else 2

    anywhere = pl.BlockSpec(memory_space=pl.ANY)
    vmem = pl.BlockSpec(memory_space=pltpu.VMEM)
    dma = pltpu.SemaphoreType.DMA

    rows_b = pb * events
    lanes = heads * events
    ff = mp * ff_part
    embed = key_embed.shape[1]
    table_lanes = -(-max(sessions, nb * slots) // 128) * 128
    grad, loss_row = pl.pallas_call(
        functools.partial(step_kernel, n, mp, group, capb, heads, nb),
        out_shape=(
            jax.ShapeDtypeStruct((sessions, ev_part, width), F32),
            jax.ShapeDtypeStruct((1, 128), F32),
        ),
        in_specs=[anywhere] * 11,
        out_specs=(vmem,) * 2,
        scratch_shapes=[
            pltpu.SMEM((total,), jnp.int32),
            pltpu.SMEM((total,), jnp.int32),
            pltpu.SMEM((sessions,), jnp.int32),
            pltpu.VMEM((1, total), jnp.int32),
            pltpu.VMEM((sessions, ev_part, width), BF16),
            pltpu.VMEM((width, embed), BF16),
            pltpu.VMEM((n, sessions), jnp.int32),
            pltpu.VMEM((8 + n, table_lanes), jnp.int32),
            pltpu.SMEM((8 + n, table_lanes), jnp.int32),
            pltpu.VMEM((nb * slots, ev_part, width), BF16),
            pltpu.VMEM((nb * slots, ev_part, width), BF16),
            pltpu.VMEM((slots, ev_part, width), BF16),
            pltpu.VMEM((sessions, ev_part, width), BF16),
            pltpu.VMEM((chunk, mp, ev_part, width), BF16),
            pltpu.VMEM((total, embed), BF16),
            pltpu.VMEM((mp, 4 * inner_part + width + ff_part, width), BF16),
            pltpu.VMEM((chunk, mp, ev_part, width), BF16),
            pltpu.VMEM((sessions, ev_part, width), BF16),
            pltpu.VMEM((wave, ev_part, width), BF16),
            pltpu.VMEM((nb * slots, ev_part, width), BF16),
            pltpu.VMEM((nb * slots, ev_part, width), BF16),
            pltpu.VMEM((nb, pb, 128), F32),
            pltpu.VMEM((mp * nb, pb, 128), F32),
            pltpu.VMEM((3 * inner, width), BF16),
            pltpu.VMEM((inner, width), BF16),
            pltpu.VMEM((total, embed), BF16),
            pltpu.VMEM((total, embed), BF16),
            pltpu.VMEM((nb, rows_b, width), F32),
            pltpu.VMEM((nb, rows_b, 128), F32),
            pltpu.VMEM((nb, rows_b, 3 * inner), BF16),
            pltpu.VMEM((nb, rows_b, lanes), F32),
            pltpu.VMEM((rows_b, ff), BF16),
            pltpu.VMEM((pb, ff), F32),
            pltpu.VMEM((pb, width), F32),
            pltpu.VMEM((nb, pb, inner), F32),
            pltpu.VMEM((nb, rows_b, inner), F32),
            pltpu.VMEM((pb, ff), F32),
            pltpu.VMEM((pb, inner), F32),
            pltpu.VMEM((pb, width), F32),
            pltpu.VMEM((nb, 4, pb, 128), F32),
            pltpu.SMEM((chunk,), jnp.int32),
            dma((nb, n)), dma((nb, n)), dma((n,)), dma((n,)),
            dma((nb, mp)), dma((nb, mp)), dma((3, mp)), dma((3, mp)),
            dma((3, mp, group)), dma((3, mp, group)), dma((3, mp)), dma((3, mp)),
            dma((nb, mp)), dma((nb, mp)), dma((mp,)), dma((mp,)),
            dma((nb, n)), dma((nb, n)), dma((7,)), dma((6,)), dma(()),
        ],
        compiler_params=pltpu.CompilerParams(
            collective_id=0, has_side_effects=True, vmem_limit_bytes=56 * 1024 * 1024
        ),
    )(
        partner, partner.reshape(1, total), lengths, mix_numer,
        states, key_embed, w_qkv.transpose(0, 2, 1), w_out, w_up, w_down, w_proj,
    )
    parts = 4 if sessions % 4 == 0 else 1
    grad, loss_row = pl.pallas_call(
        functools.partial(hand_over, parts),
        out_shape=(
            jax.ShapeDtypeStruct(grad.shape, F32),
            jax.ShapeDtypeStruct((1, sessions), F32),
        ),
        in_specs=[anywhere, vmem],
        out_specs=(anywhere, vmem),
        scratch_shapes=[pltpu.VMEM(grad.shape, F32), dma((parts,)), dma((parts,))],
    )(grad, loss_row)
    return (loss_row.reshape(sessions), grad)


def solution(mesh):
    placed = (
        P("dp", "mp", None),
        P("dp", None),
        P(),
        P("dp"),
        P(),
        P(None, None, "mp"),
        P("mp", None),
        P(None, "mp"),
        P("mp", None),
        P(),
    )
    return jax.shard_map(
        local, mesh=mesh, in_specs=placed, out_specs=(P("dp"), P("dp", "mp", None)), check_vma=False
    )
```

```python
import functools

import jax
import jax.numpy as jnp
from jax import lax
from jax.experimental import pallas as pl
from jax.experimental.pallas import tpu as pltpu
from jax.sharding import PartitionSpec as P

HD = 64
SOFTMAX_TEMP = 0.1
LN_EPS = 1e-05
NORM_EPS = 1e-06
MESH = pl.DeviceIdType.MESH
F32 = jnp.float32
BF16 = jnp.bfloat16


def remote(src, dst, send_sem, recv_sem, device):
    return pltpu.make_async_remote_copy(
        src_ref=src,
        dst_ref=dst,
        send_sem=send_sem,
        recv_sem=recv_sem,
        device_id=device,
        device_id_type=MESH,
    )


def signal_all(n, mp):
    me, mz = lax.axis_index("dp"), lax.axis_index("mp")
    barrier = pltpu.get_barrier_semaphore()
    for o in range(1, n):
        pl.semaphore_signal(
            barrier, inc=1, device_id={"dp": lax.rem(me + o, n)}, device_id_type=MESH
        )
    for o in range(1, mp):
        pl.semaphore_signal(
            barrier, inc=1, device_id={"mp": lax.rem(mz + o, mp)}, device_id_type=MESH
        )


def wait_all(n, mp):
    pl.semaphore_wait(pltpu.get_barrier_semaphore(), n - 1 + mp - 1)


def dot(a, b, ca=1, cb=0):
    return lax.dot_general(
        a, b, (((ca,), (cb,)), ((), ())), preferred_element_type=F32
    )


def halves(a):
    hi = a.astype(BF16)
    return hi, (a - hi.astype(F32)).astype(BF16)


def dot_split(a, b, cb=0):
    rows = a.shape[0]
    both = dot(jnp.concatenate(halves(a), axis=0), b, 1, cb)
    return both[0:rows] + both[rows : 2 * rows]


def dot_both(a, b_hi, b_lo, cb=0):
    return dot_split(a, b_hi, cb) + dot(a.astype(BF16), b_lo, 1, cb)


def over(x, k):
    return x >> (k.bit_length() - 1) if k & (k - 1) == 0 else x // k


def make_tables(n, mp, nb, capb, sessions, row_v, source_v, table_v):
    me = lax.axis_index("dp")
    slots = n * capb
    wave = sessions // nb
    lanes = table_v.shape[1]
    row = row_v[...]
    partner = jnp.concatenate(
        [row[:, d * sessions : (d + 1) * sessions] for d in range(n)], axis=0
    )
    source = over(partner, sessions)
    source_v[...] = source
    rel = partner - me * sessions
    mine = source == me
    i_sub = lax.broadcasted_iota(jnp.int32, (sessions, sessions), 0)
    i_lane = lax.broadcasted_iota(jnp.int32, (sessions, sessions), 1)
    here = jnp.where(mine, 1, 0)
    seen, step = here, 1
    while step < sessions:
        zeros = jnp.zeros((n, step), jnp.int32)
        seen = seen + jnp.concatenate([zeros, seen[:, : sessions - step]], axis=1)
        step *= 2
    slot = seen - here
    rank = slot + jnp.sum(jnp.where(source < me, 1, 0), axis=1, keepdims=True)
    wave_of = rank - over(rank, nb) * nb
    depth = over(slot, nb)
    cell = wave_of * capb + depth
    cell_lane = lax.broadcasted_iota(jnp.int32, (n, lanes), 1)
    send = jnp.zeros((n, lanes), jnp.int32)
    for c in range(nb * capb):
        value = jnp.sum(jnp.where(mine & (cell == c), rel, 0), axis=1, keepdims=True)
        send = jnp.where(cell_lane == c, value, send)
    table_v[8 : 8 + n, :] = jnp.clip(send, 0, sessions - 1)

    peer = lax.broadcasted_iota(jnp.int32, (n, sessions), 0)
    code = wave_of * slots + peer * capb + depth
    found = jnp.zeros((sessions, sessions), jnp.int32)
    for d in range(n):
        found = found + jnp.where(rel[d : d + 1] == i_sub, code[d : d + 1], 0)
    send_code = jnp.sum(found, axis=1, keepdims=True)

    own = source_v[pl.ds(me, 1), :]
    own_col = jnp.sum(jnp.where(i_sub == i_lane, own, 0), axis=1, keepdims=True)
    slot_col = jnp.sum(
        jnp.where((own_col == own) & (i_lane < i_sub), 1, 0), axis=1, keepdims=True
    )
    rank_col = slot_col + jnp.sum(jnp.where(own < own_col, 1, 0), axis=1, keepdims=True)
    t_col = over(rank_col, nb)
    b_col = rank_col - t_col * nb
    at_col = b_col * wave + t_col
    in_col = own_col * capb + over(slot_col, nb)
    code_col = b_col * slots + in_col
    wide_lane = lax.broadcasted_iota(jnp.int32, (sessions, lanes), 1)
    wide_sub = lax.broadcasted_iota(jnp.int32, (sessions, lanes), 0)

    def scatter(col, value, count):
        total = jnp.sum(jnp.where(col == wide_lane, value, 0), axis=0, keepdims=True)
        return jnp.clip(total, 0, count - 1)

    table_v[0:1, :] = scatter(at_col, wide_sub, sessions)
    table_v[1:2, :] = scatter(at_col, in_col, slots)
    table_v[2:3, :] = scatter(wide_sub, at_col, sessions)
    table_v[3:4, :] = scatter(wide_sub, send_code, nb * slots)
    table_v[4:5, :] = scatter(code_col, t_col, wave)
    table_v[5:8, :] = jnp.zeros((3, lanes), jnp.int32)


def step_kernel(
    n, mp, group, capb, heads, nb,
    partner_in, partner_row, lengths_in, mix_in,
    states_in, keys_in, w_qkv_in, w_out_in, w_up_in, w_down_in, w_proj_in,
    grad, loss_out,
    partner, lengths, mix_num, row_v, states, w_proj, source_v, table_v, table,
    out_buf, in_buf, in_now, mix_buf, mixed, all_keys, all_wts,
    dmix, dm_home, dm_now, ret_buf, arr, loss, all_loss,
    wqkv, w_out, key_hi, key_lo, unit_s, inv_s, proj, probs, slope, hpool, xpool, ctx, seen_s,
    d_hid, d_ctx, g_row, aux, lens,
    dp_s, dp_r, key_s, key_r, mp_s, mp_r, wz_s, wz_r, wg_s, wg_r, wc_s, wc_r,
    zo_s, zo_r, ls_s, ls_r, do_s, do_r, in_sem, w_sem, table_sem,
):
    me, mz = lax.axis_index("dp"), lax.axis_index("mp")
    sessions, ev_part, width = states.shape
    chunk = sessions // mp
    pb = chunk // nb
    wave = mp * pb
    slots = n * capb
    events = ev_part * mp
    part_w = w_out_in.shape[0]
    inner = part_w * mp
    ff_part = w_up_in.shape[1]
    lanes = heads * events
    rows_b = pb * events
    up0 = 4 * part_w
    down0 = up0 + width
    z_order = (2, 1, 3) if mp == 4 else tuple(range(1, mp))

    signal_all(n, mp)

    chips = group // 2
    place = lax.rem(me, group)
    base = me - place
    core = lax.rem(place, 2)
    chip = place // 2
    key_rows = pl.ds(pl.multiple_of(me * sessions, sessions), sessions)
    loads = [
        pltpu.make_async_copy(src, dst, in_sem.at[i])
        for i, (src, dst) in enumerate(
            [
                (partner_row, row_v),
                (partner_in, partner),
                (lengths_in, lengths),
                (mix_in, mix_num),
                (states_in, states),
                (keys_in, all_keys.at[key_rows]),
                (w_proj_in, w_proj),
            ]
        )
    ]
    w_loads = [
        pltpu.make_async_copy(src, all_wts.at[mz, pl.ds(at, src.shape[0])], w_sem.at[i])
        for i, (src, at) in enumerate(
            [(w_qkv_in.at[j], j * part_w) for j in range(3)]
            + [(w_out_in, 3 * part_w), (w_up_in, up0), (w_down_in, down0)]
        )
    ]
    loads[0].start()
    for c in w_loads:
        c.start()
    for c in loads[1:]:
        c.start()
    loads[0].wait()
    make_tables(n, mp, nb, capb, sessions, row_v, source_v, table_v)
    table_copy = pltpu.make_async_copy(table_v, table, table_sem)
    table_copy.start()

    def order(p):
        return table[0, p]

    for c in w_loads:
        c.wait()
    loads[5].wait()
    wait_all(n, mp)

    def dp_in(b, o):
        peer = lax.rem(me + o, n)
        return remote(
            out_buf.at[pl.ds(b * slots + peer * capb, capb)],
            in_buf.at[pl.ds(b * slots + me * capb, capb)],
            dp_s.at[b, o], dp_r.at[b, o], {"dp": peer},
        )

    def z_in(b, o):
        peer = lax.rem(mz + o, mp)
        return remote(
            mix_buf.at[pl.ds(b * wave + peer * pb, pb)],
            mixed.at[pl.ds(b * pb, pb), mz],
            mp_s.at[b, o], mp_r.at[b, o], {"mp": peer},
        )

    def z_out(b, o):
        peer = lax.rem(mz + o, mp)
        return remote(
            dmix.at[pl.ds(b * pb, pb), peer],
            dm_home.at[pl.ds(b * wave + mz * pb, pb)],
            zo_s.at[b, o], zo_r.at[b, o], {"mp": peer},
        )

    def dp_out(b, o):
        peer = lax.rem(me + o, n)
        return remote(
            ret_buf.at[pl.ds(b * slots + peer * capb, capb)],
            arr.at[pl.ds(b * slots + me * capb, capb)],
            do_s.at[b, o], do_r.at[b, o], {"dp": peer},
        )

    sizes = (4 * part_w, width, ff_part)
    offsets = (0, up0, down0)

    def w_rows(g, first, count):
        piece = sizes[g] // group
        return pl.ds(pl.multiple_of(offsets[g] + first * piece, piece), count * piece)

    def w_z(g, o):
        part = all_wts.at[mz, w_rows(g, core * chips + chip, 1)]
        return remote(part, part, wz_s.at[g, o], wz_r.at[g, o], {"mp": lax.rem(mz + o, mp)})

    def w_plane(g, o, h):
        part = all_wts.at[lax.rem(mz + mp - o, mp), w_rows(g, core * chips + chip, 1)]
        peer = base + lax.rem(chip + h, chips) * 2 + core
        return remote(part, part, wg_s.at[g, o, h], wg_r.at[g, o, h], {"dp": peer})

    def w_core(g, o):
        part = all_wts.at[lax.rem(mz + mp - o, mp), w_rows(g, core * chips, chips)]
        return remote(part, part, wc_s.at[g, o], wc_r.at[g, o], {"dp": me + 1 - 2 * core})

    def spread_weights(g):
        for o in range(1, mp):
            w_z(g, o).wait()
            for h in range(1, chips):
                w_plane(g, o, h).start()

    def swap_weights(g):
        for o in range(1, mp):
            for h in range(1, chips):
                w_plane(g, o, h).wait()
            w_core(g, o).start()

    def have_weights(g):
        for o in range(1, mp):
            w_core(g, o).wait()

    def send_out(b):
        @pl.loop(0, n, unroll=2)
        def _(d):
            for k in range(capb):
                out_buf[b * slots + d * capb + k] = states[table[8 + d, b * capb + k]]

        for o in range(1, n):
            dp_in(b, o).start()

    def mix(b):
        for o in range(1, n):
            dp_in(b, o).wait()
        in_now[...] = in_buf[pl.ds(b * slots, slots)]

        @pl.loop(0, wave, unroll=8)
        def _(t):
            i = order(b * wave + t)
            w = mix_num[i].astype(F32) * 0.0625
            mix_buf[b * wave + t] = (
                w * states[i].astype(F32)
                + (1.0 - w) * in_now[table[1, b * wave + t]].astype(F32)
            ).astype(BF16)

        for o in z_order:
            z_in(b, o).start()
        mixed[b * pb : (b + 1) * pb, mz] = mix_buf[pl.ds(b * wave + mz * pb, pb)]

    key_copies = [
        remote(
            all_keys.at[key_rows], all_keys.at[key_rows], key_s.at[o], key_r.at[o],
            {"dp": lax.rem(me + o, n)},
        )
        for o in range(1, n)
    ]
    for g in range(3):
        for o in range(1, mp):
            w_z(g, o).start()
    for c in loads[1:5] + loads[6:]:
        c.wait()
    table_copy.wait()
    ahead = min(2, nb)
    for b in range(ahead):
        send_out(b)
    for b in range(nb):
        for s in range(pb):
            i = b * pb + s
            own = order(b * wave + mz * pb + s)
            other = partner[me * sessions + own]
            longest = jnp.maximum(lengths[me * sessions + own], lengths[other])
            lens[i] = longest
            row = slice(s, s + 1)
            shape = (1, aux.shape[3])
            aux[b, 0, row, :] = jnp.full(shape, mix_num[own].astype(F32) * 0.0625, F32)
            aux[b, 1, row, :] = jnp.full(shape, longest.astype(F32), F32)
            aux[b, 2, row, :] = jnp.full(shape, own.astype(F32), F32)
            aux[b, 3, row, :] = jnp.full(shape, other.astype(F32), F32)
    spread_weights(0)
    mix(0)
    spread_weights(1)
    mix(1)
    spread_weights(2)
    for c in key_copies:
            c.start()
    for b in range(ahead, nb):
            send_out(b)
    swap_weights(0)

    head_mask = (
        lax.broadcasted_iota(jnp.int32, (lanes, inner), 0) // events
        == lax.broadcasted_iota(jnp.int32, (lanes, inner), 1) // HD
    )
    ones_blk = head_mask.astype(F32).astype(BF16)
    row_t = lax.broadcasted_iota(jnp.int32, (events, lanes), 0)
    lane_t = lax.broadcasted_iota(jnp.int32, (events, lanes), 1) % events
    row_w = lax.broadcasted_iota(jnp.int32, (events, width), 0)
    col_head = lax.broadcasted_iota(jnp.int32, (events, inner), 1) // HD
    pool_row = lax.broadcasted_iota(jnp.int32, (pb, rows_b), 0)
    pool_lane = lax.broadcasted_iota(jnp.int32, (pb, rows_b), 1)
    zero_b = jnp.zeros((lanes, inner), BF16)
    scale = HD ** (-0.5)
    c0 = 0.7978845608028654
    c1 = c0 * 0.044715

    def spread(v):
        return jnp.where(head_mask, jnp.concatenate([v] * heads, axis=0), zero_b)

    def fold(full):
        total = full[0:events]
        for h in range(1, heads):
            total = jnp.where(col_head == h, full[h * events : (h + 1) * events], total)
        return total

    def attend(b):
        mixed_b = mixed[pl.ds(b * pb, pb)].reshape(rows_b, width)
        x = mixed_b.astype(F32)
        centered = x - jnp.mean(x, axis=1, keepdims=True)
        inv = lax.rsqrt(jnp.mean(centered * centered, axis=1, keepdims=True) + LN_EPS)
        unit = centered * inv
        unit_s[b] = unit
        inv_s[b] = jnp.broadcast_to(inv, inv_s.shape[1:])
        qkv = dot(unit.astype(BF16), wqkv[...], 1, 1).astype(BF16)
        proj[b] = qkv
        used = []
        for s in range(pb):
            length = lens[b * pb + s]
            lo = s * events
            q = qkv[lo : lo + events, 0:inner]
            k = qkv[lo : lo + events, inner : 2 * inner]
            e = jnp.where(row_t < length, jnp.exp(dot(k, spread(q), 1, 1) * scale), 0.0)
            p = e * (1.0 / jnp.sum(e, axis=0, keepdims=True))
            probs[b, lo : lo + events, :] = p
            used.append(jnp.where(lane_t < length, p, 0.0).astype(BF16))
        seen = dot(jnp.concatenate(used, axis=0), ones_blk)
        seen_s[b] = seen
        for s in range(pb):
            lo = s * events
            v = qkv[lo : lo + events, 2 * inner : 3 * inner].astype(F32)
            ctx[b, s : s + 1, :] = jnp.sum(
                seen[lo : lo + events] * v, axis=0, keepdims=True
            ) / lens[b * pb + s].astype(F32)

    def feed(b):
        len_col = aux[b, 1, :, 0:1]
        pool_mask = jnp.where(
            (pool_lane // events == pool_row)
            & ((pool_lane % events).astype(F32) < len_col),
            1.0,
            0.0,
        ).astype(BF16)
        xpool[b] = dot(pool_mask, mixed[pl.ds(b * pb, pb)].reshape(rows_b, width)) / len_col
        normed = unit_s[b].astype(BF16)
        for m in range(mp):
            pre = dot(normed, all_wts[m, up0 : up0 + width, :])
            sq = pre * pre
            side = 0.5 + 0.5 * jnp.tanh(pre * (c0 + c1 * sq))
            act = pre * side
            cols = slice(m * ff_part, (m + 1) * ff_part)
            slope[b, :, cols] = (
                side + act * (1.0 - side) * (2.0 * c0 + (6.0 * c1) * sq)
            ).astype(BF16)
            hpool[b, :, cols] = dot(pool_mask, act.astype(BF16)) / len_col

    def contrast(lo, hi):
        def stack(part):
            return jnp.concatenate([part(b) for b in range(lo, hi)], axis=0)

        def unstack(ref, value):
            for b in range(lo, hi):
                ref[b] = value[(b - lo) * pb : (b - lo + 1) * pb]

        weight, len_all, own, partner_id = (
            stack(lambda b: aux[b, j, :, 0:1]) for j in range(4)
        )
        own_id = own + (me * sessions).astype(F32)
        pooled = stack(lambda b: xpool[b]) + dot_split(stack(lambda b: ctx[b]), w_out[...])
        for m in range(mp):
            cols = slice(m * ff_part, (m + 1) * ff_part)
            pooled = pooled + dot_split(
                stack(lambda b: hpool[b, :, cols]), all_wts[m, down0 : down0 + ff_part, :]
            )
        embed = dot_split(pooled, w_proj[...])
        inv_norm = lax.rsqrt(jnp.sum(embed * embed, axis=1, keepdims=True) + NORM_EPS)
        unit_q = embed * inv_norm
        logits = dot_both(unit_q, key_hi[...], key_lo[...], 1) / SOFTMAX_TEMP
        exp_l = jnp.exp(logits)
        sum_l = jnp.sum(exp_l, axis=1, keepdims=True)
        ids = lax.broadcasted_iota(jnp.int32, logits.shape, 1).astype(F32)
        wanted = jnp.where(ids == own_id, weight, 0.0) + jnp.where(
            ids == partner_id, 1.0 - weight, 0.0
        )
        mine = (
            lax.broadcasted_iota(jnp.int32, (own.shape[0], loss.shape[2]), 1).astype(F32) == own
        )
        value = jnp.log(sum_l) - jnp.sum(wanted * logits, axis=1, keepdims=True)
        unstack(loss, jnp.where(mine, value, 0.0))
        grad_u = dot_both(exp_l / sum_l - wanted, key_hi[...], key_lo[...]) / SOFTMAX_TEMP
        grad_e = (
            grad_u - unit_q * jnp.sum(unit_q * grad_u, axis=1, keepdims=True)
        ) * inv_norm
        g = dot_split(grad_e, w_proj[...], 1) * (1.0 / len_all)
        unstack(g_row, g)
        g_b = g.astype(BF16)
        for m in range(mp):
            d_part = dot(g_b, all_wts[m, down0 : down0 + ff_part, :], 1, 1)
            for b in range(lo, hi):
                d_hid[b, :, m * ff_part : (m + 1) * ff_part] = d_part[
                    (b - lo) * pb : (b - lo + 1) * pb
                ]
        unstack(d_ctx, dot(g_b, w_out[...], 1, 1).astype(BF16).astype(F32))

    def backward(b):
        along_v = []
        for s in range(pb):
            lo = s * events
            v = proj[b, lo : lo + events, 2 * inner : 3 * inner].astype(F32)
            along_v.append((v * d_ctx[b, s : s + 1, :]).astype(BF16))
        u_all = dot(jnp.concatenate(along_v, axis=0), ones_blk, 1, 1)
        d_q, d_k, d_v = [], [], []
        for s in range(pb):
            length = lens[b * pb + s]
            lo = s * events
            q = proj[b, lo : lo + events, 0:inner]
            k = proj[b, lo : lo + events, inner : 2 * inner]
            p = probs[b, lo : lo + events, :]
            u = u_all[lo : lo + events]
            total = jnp.sum(p * u, axis=0, keepdims=True)
            d_score = jnp.where(lane_t < length, p * (u - total) * scale, 0.0).astype(BF16)
            d_k.append(dot(d_score, spread(q)).astype(BF16))
            d_q.append(fold(dot(d_score, k, 0, 0)).astype(BF16))
            d_v.append((seen_s[b, lo : lo + events, :] * d_ctx[b, s : s + 1, :]).astype(BF16))
        dn = dot(jnp.concatenate(d_q, axis=0), wqkv[0:inner, :])
        dn = dn + dot(jnp.concatenate(d_k, axis=0), wqkv[inner : 2 * inner, :])
        dn = dn + dot(jnp.concatenate(d_v, axis=0), wqkv[2 * inner : 3 * inner, :])
        for m in range(mp):
            cols = slice(m * ff_part, (m + 1) * ff_part)
            d_pre = jnp.concatenate(
                [
                    (
                        slope[b, s * events : (s + 1) * events, cols].astype(F32)
                        * d_hid[b, s : s + 1, cols]
                    ).astype(BF16)
                    for s in range(pb)
                ],
                axis=0,
            )
            dn = dn + dot(d_pre, all_wts[m, up0 : up0 + width, :], 1, 1)
        unit = unit_s[b]
        center = jnp.mean(dn, axis=1, keepdims=True)
        along = jnp.mean(dn * unit, axis=1, keepdims=True)
        body = (dn - center - unit * along) * inv_s[b, :, 0:1]
        for s in range(pb):
            d_mixed = jnp.where(
                row_w < lens[b * pb + s],
                g_row[b, s : s + 1, :] + body[s * events : (s + 1) * events],
                0.0,
            )
            dmix[b * pb + s] = d_mixed.astype(BF16).reshape(mp, ev_part, width)

    def give_back(b):
        for o in range(1, mp):
            z_out(b, o).wait()
        dm_now[...] = dm_home[pl.ds(b * wave, wave)]

        @pl.loop(0, slots, unroll=8)
        def _(j):
            t = table[4, b * slots + j]
            w = mix_num[order(b * wave + t)].astype(F32) * 0.0625
            ret_buf[b * slots + j] = ((1.0 - w) * dm_now[t].astype(F32)).astype(BF16)

        for o in range(1, n):
            dp_out(b, o).start()

    def arrived(b):
        for o in range(1, mp):
            z_in(b, o).wait()

    have_weights(0)
    for m in range(mp):
        for j in range(3):
            wqkv[j * inner + m * part_w : j * inner + (m + 1) * part_w, :] = all_wts[
                m, j * part_w : (j + 1) * part_w, :
            ]
        w_out[m * part_w : (m + 1) * part_w, :] = all_wts[m, 3 * part_w : 4 * part_w, :]
    arrived(0)
    attend(0)
    swap_weights(1)
    for b in range(ahead, min(3, nb)):
        mix(b)
    if nb > 1:
        arrived(1)
        attend(1)
    swap_weights(2)
    for b in range(3, nb):
        mix(b)
    for c in key_copies:
        c.wait()
    keys_f = all_keys[...].astype(F32)
    unit_k = keys_f * lax.rsqrt(jnp.sum(keys_f * keys_f, axis=1, keepdims=True) + NORM_EPS)
    k_hi, k_lo = halves(unit_k)
    key_hi[...] = k_hi
    key_lo[...] = k_lo
    have_weights(1)
    have_weights(2)

    groups = ((0, 2), (2, 3), (3, 4)) if nb == 4 else ((0, nb),)
    done = ahead
    back = 0
    for lo, hi in groups:
        for b in range(done, hi):
            arrived(b)
            attend(b)
        done = max(done, hi)
        for b in range(lo, hi):
            feed(b)
        contrast(lo, hi)
        for b in range(lo, hi):
            backward(b)
            for o in z_order:
                z_out(b, o).start()
            dm_home[pl.ds(b * wave + mz * pb, pb)] = dmix[pl.ds(b * pb, pb), mz]
            if back < lo:
                give_back(back)
                back += 1
    for b in range(back, nb - 1):
        give_back(b)

    loss_copies = []
    for o in range(1, mp):
        c = remote(
            loss, all_loss.at[pl.ds(mz * nb, nb)],
            ls_s.at[o], ls_r.at[o], {"mp": lax.rem(mz + o, mp)},
        )
        c.start()
        loss_copies.append(c)
    all_loss[pl.ds(mz * nb, nb)] = loss[...]
    give_back(nb - 1)
    for c in loss_copies:
        c.wait()
    loss_out[...] = jnp.sum(jnp.sum(all_loss[...], axis=0), axis=0, keepdims=True)
    for b in range(nb):
        for o in range(1, n):
            dp_out(b, o).wait()

    @pl.loop(0, sessions, unroll=8)
    def _(i):
        grad[i] = (
            mix_num[i].astype(F32) * 0.0625 * dm_home[table[2, i]].astype(F32)
            + arr[table[3, i]].astype(F32)
        )


def hand_over(parts, grad_in, loss_in, grad, loss, held, in_sem, out_sem):
    block = grad.shape[0] // parts
    ins, outs = [], []
    for i in range(parts):
        rows = pl.ds(i * block, block)
        ins.append(pltpu.make_async_copy(grad_in.at[rows], held.at[rows], in_sem.at[i]))
        outs.append(pltpu.make_async_copy(held.at[rows], grad.at[rows], out_sem.at[i]))
        ins[i].start()
    loss[...] = loss_in[:, 0 : loss.shape[1]]
    for i in range(parts):
        ins[i].wait()
        outs[i].start()
    for i in range(parts):
        outs[i].wait()


def local(states, key_embed, partner, mix_numer, lengths, w_qkv, w_out, w_up, w_down, w_proj):
    sessions, ev_part, width = states.shape
    n = lax.axis_size("dp")
    mp = lax.axis_size("mp")
    cap = (sessions + n - 2) // (n - 1)
    me = lax.axis_index("dp")
    total = partner.shape[0]
    chunk = sessions // mp
    nb = 4 if chunk % 4 == 0 else 1
    pb = chunk // nb
    wave = mp * pb
    capb = (cap + nb - 1) // nb
    slots = n * capb
    events = ev_part * mp
    inner_part = w_qkv.shape[2]
    inner = inner_part * mp
    heads = inner // HD
    ff_part = w_up.shape[1]
    group = 8 if n % 8 == 0 else 2

    anywhere = pl.BlockSpec(memory_space=pl.ANY)
    vmem = pl.BlockSpec(memory_space=pltpu.VMEM)
    dma = pltpu.SemaphoreType.DMA

    rows_b = pb * events
    lanes = heads * events
    ff = mp * ff_part
    embed = key_embed.shape[1]
    table_lanes = -(-max(sessions, nb * slots) // 128) * 128
    grad, loss_row = pl.pallas_call(
        functools.partial(step_kernel, n, mp, group, capb, heads, nb),
        out_shape=(
            jax.ShapeDtypeStruct((sessions, ev_part, width), F32),
            jax.ShapeDtypeStruct((1, 128), F32),
        ),
        in_specs=[anywhere] * 11,
        out_specs=(vmem,) * 2,
        scratch_shapes=[
            pltpu.SMEM((total,), jnp.int32),
            pltpu.SMEM((total,), jnp.int32),
            pltpu.SMEM((sessions,), jnp.int32),
            pltpu.VMEM((1, total), jnp.int32),
            pltpu.VMEM((sessions, ev_part, width), BF16),
            pltpu.VMEM((width, embed), BF16),
            pltpu.VMEM((n, sessions), jnp.int32),
            pltpu.VMEM((8 + n, table_lanes), jnp.int32),
            pltpu.SMEM((8 + n, table_lanes), jnp.int32),
            pltpu.VMEM((nb * slots, ev_part, width), BF16),
            pltpu.VMEM((nb * slots, ev_part, width), BF16),
            pltpu.VMEM((slots, ev_part, width), BF16),
            pltpu.VMEM((sessions, ev_part, width), BF16),
            pltpu.VMEM((chunk, mp, ev_part, width), BF16),
            pltpu.VMEM((total, embed), BF16),
            pltpu.VMEM((mp, 4 * inner_part + width + ff_part, width), BF16),
            pltpu.VMEM((chunk, mp, ev_part, width), BF16),
            pltpu.VMEM((sessions, ev_part, width), BF16),
            pltpu.VMEM((wave, ev_part, width), BF16),
            pltpu.VMEM((nb * slots, ev_part, width), BF16),
            pltpu.VMEM((nb * slots, ev_part, width), BF16),
            pltpu.VMEM((nb, pb, 128), F32),
            pltpu.VMEM((mp * nb, pb, 128), F32),
            pltpu.VMEM((3 * inner, width), BF16),
            pltpu.VMEM((inner, width), BF16),
            pltpu.VMEM((total, embed), BF16),
            pltpu.VMEM((total, embed), BF16),
            pltpu.VMEM((nb, rows_b, width), F32),
            pltpu.VMEM((nb, rows_b, 128), F32),
            pltpu.VMEM((nb, rows_b, 3 * inner), BF16),
            pltpu.VMEM((nb, rows_b, lanes), F32),
            pltpu.VMEM((nb, rows_b, ff), BF16),
            pltpu.VMEM((nb, pb, ff), F32),
            pltpu.VMEM((nb, pb, width), F32),
            pltpu.VMEM((nb, pb, inner), F32),
            pltpu.VMEM((nb, rows_b, inner), F32),
            pltpu.VMEM((nb, pb, ff), F32),
            pltpu.VMEM((nb, pb, inner), F32),
            pltpu.VMEM((nb, pb, width), F32),
            pltpu.VMEM((nb, 4, pb, 128), F32),
            pltpu.SMEM((chunk,), jnp.int32),
            dma((nb, n)), dma((nb, n)), dma((n,)), dma((n,)),
            dma((nb, mp)), dma((nb, mp)), dma((3, mp)), dma((3, mp)),
            dma((3, mp, group)), dma((3, mp, group)), dma((3, mp)), dma((3, mp)),
            dma((nb, mp)), dma((nb, mp)), dma((mp,)), dma((mp,)),
            dma((nb, n)), dma((nb, n)), dma((7,)), dma((6,)), dma(()),
        ],
        compiler_params=pltpu.CompilerParams(
            collective_id=0, has_side_effects=True, vmem_limit_bytes=56 * 1024 * 1024
        ),
    )(
        partner, partner.reshape(1, total), lengths, mix_numer,
        states, key_embed, w_qkv.transpose(0, 2, 1), w_out, w_up, w_down, w_proj,
    )
    parts = 4 if sessions % 4 == 0 else 1
    grad, loss_row = pl.pallas_call(
        functools.partial(hand_over, parts),
        out_shape=(
            jax.ShapeDtypeStruct(grad.shape, F32),
            jax.ShapeDtypeStruct((1, sessions), F32),
        ),
        in_specs=[anywhere, vmem],
        out_specs=(anywhere, vmem),
        scratch_shapes=[pltpu.VMEM(grad.shape, F32), dma((parts,)), dma((parts,))],
    )(grad, loss_row)
    return (loss_row.reshape(sessions), grad)


def solution(mesh):
    placed = (
        P("dp", "mp", None),
        P("dp", None),
        P(),
        P("dp"),
        P(),
        P(None, None, "mp"),
        P("mp", None),
        P(None, "mp"),
        P("mp", None),
        P(),
    )
    return jax.shard_map(
        local, mesh=mesh, in_specs=placed, out_specs=(P("dp"), P("dp", "mp", None)), check_vma=False
    )
```
